128 devices in a mesh: sn: 32 (over x, y, core), rhs: 4 (over z).
Axes of the slice: x: 4, y: 4, z: 4, core: 2. Of those that a mesh axis runs over, the one named last changes fastest.
Arguments:
- rhs_leaf: float32 [1024, 256, 128], P('sn', 'rhs'), may hold values from -6 to 6
- rhs_top: float32 [32, 256, 128], P('sn', 'rhs'), may hold values from -6 to 6
- leaf_blocks: float32 [1024, 3, 128, 128], P('sn', None, 'rhs'), may hold values from -0.078125 to 0.078125
- leaf_dinv: float32 [1024, 128, 128], P('sn', 'rhs')
- leaf_struct: int32 [1024, 3], P('sn'), may hold values from 1 to 63, as said below
- top_blocks: float32 [32, 32, 128, 128], P(None, 'sn', 'rhs'), may hold values from -0.1875 to 0.1875
- top_dinv: float32 [32, 128, 128], P('sn', 'rhs')
Outputs:
- leaf_solution: float32 [1024, 256, 128], P('sn', 'rhs')
- top_solution: float32 [32, 256, 128], P('sn', 'rhs')
The draws below stay inside these ranges and needn't reach their ends.
Inputs may be any that keep to these rules, and one draw needn't show every extreme that they name: `leaf_struct`: subtree d hangs below top supernode a = 4 * (d // 4). Row d * 32 + s names 3 distinct ancestors of leaf supernode s of subtree d: a value v < 32 is supernode v of the same subtree, with v > s; a value 32 + k is a top supernode k on a's path to the root, that is k = a or the factor holds top block (k, a). Column 0 is the elimination tree parent: s + 1, except for the subtree's last supernode, whose parent is 32 + a.
All inputs are finite; a program needn't handle non-finite values.
Results may differ from the reference program's by a relative error of at most 0.00018.
Values sent between devices are 32-bit elements; how exact they have to be, the bound alone decides.
A program may use at most 64 MiB of HBM per device.

```python
from functools import partial
import jax
import jax.numpy as jnp
from jax import lax

W = 128
NRHS = 256
R = 3
LEAF = 32
TOPS = 32
LEAFS = 1024


def dominant_inverse(key, count):
    diag_key, off_key = jax.random.split(key)
    diagonal = jax.random.uniform(diag_key, (count, W), jnp.float32, 0.7, 1.3)
    off_part = jnp.clip(jax.random.normal(off_key, (count, W, W), jnp.float32), -4.0, 4.0) * (0.35 / W ** 0.5)
    identity_mask = jnp.eye(W, dtype=jnp.float32)
    return identity_mask[None] * diagonal[:, :, None] + (1.0 - identity_mask[None]) * off_part


def draw_leaf_dinv(key, part):
    return dominant_inverse(jax.random.fold_in(key, 11), LEAFS)


def draw_top_dinv(key, part):
    return dominant_inverse(jax.random.fold_in(key, 23), TOPS)


def draw_leaf_struct(key, part):
    total_nodes = LEAF + TOPS
    row_keys = jax.random.split(jax.random.fold_in(key, 37), LEAFS)
    candidate = jnp.arange(total_nodes, dtype=jnp.int32)
    top_index = jnp.clip(candidate - LEAF, 0, TOPS - 1).astype(jnp.int32)
    span = jnp.ones((total_nodes,), jnp.int32)
    for place in range(TOPS.bit_length()):
        span = span + ((top_index + 1) % 2 ** (place + 1) == 0).astype(jnp.int32) * 2 ** place
    rows = jnp.arange(LEAFS, dtype=jnp.int32)
    position = rows % LEAF
    attach = (4 * (rows // LEAF // 4)).astype(jnp.int32)
    parent = jnp.where(position < LEAF - 1, position + 1, LEAF + attach).astype(jnp.int32)

    def choose(row_key, place, parent_id, attach_top):
        scores = jax.random.permutation(row_key, total_nodes).astype(jnp.int32)
        on_path = (candidate >= LEAF) & (top_index >= attach_top) & (top_index + 1 - span <= attach_top)
        inside = (candidate > place) & (candidate < LEAF)
        allowed = (inside | on_path) & (candidate != parent_id)
        scores = jnp.where(allowed, scores, -1)
        unused, chosen = lax.top_k(scores, R - 1)
        return jnp.concatenate([parent_id[None], chosen.astype(jnp.int32)]).astype(jnp.int32)
    return jax.vmap(choose)(row_keys, position, parent, attach)


def shard_levels(own_key, dims, cuts, least, top_value):
    def one(axis_at, blocks):
        steps = jax.random.uniform(jax.random.fold_in(jax.random.fold_in(own_key, 6), axis_at), (blocks,), jnp.float32, least / len(cuts), top_value / len(cuts))
        return jnp.repeat(jnp.exp(steps), dims[axis_at] // blocks).reshape((-1,) + (1,) * (len(dims) - axis_at - 1))

    loudness = one(*cuts[0])
    for cut in cuts[1:]:
        loudness = loudness * one(*cut)
    return loudness


def bell_draw(stream_key, shape, width, reach, cuts=(), kind=jnp.bfloat16):
    entries = width * jax.random.normal(stream_key, shape, jnp.float32)
    if cuts:
        entries = entries * shard_levels(stream_key, shape, cuts, -0.22, 0.18)
    return jnp.clip(entries, -reach, reach).astype(kind)


def setup_inputs(seed: int = 0) -> dict:
    splits = jax.random.split(jax.random.key(seed), 8)
    return {
        "rhs_leaf": bell_draw(splits[0], (LEAFS, NRHS, W), 1.0, 6.0, ((0, 32), (1, 4)), jnp.float32),
        "rhs_top": bell_draw(splits[1], (TOPS, NRHS, W), 1.0, 6.0, ((0, 32), (1, 4)), jnp.float32),
        "leaf_blocks": bell_draw(splits[2], (LEAFS, R, W, W), (44 * W) ** -0.5, 0.078125, ((0, 32), (2, 4)), jnp.float32),
        "leaf_dinv": draw_leaf_dinv(jax.random.fold_in(splits[7], 71), 0),
        "leaf_struct": draw_leaf_struct(jax.random.fold_in(splits[7], 71), 0),
        "top_blocks": bell_draw(splits[5], (TOPS, TOPS, W, W), (8 * W) ** -0.5, 0.1875, ((1, 32), (2, 4)), jnp.float32),
        "top_dinv": draw_top_dinv(jax.random.fold_in(splits[7], 71), 0),
    }


highest = lax.Precision.HIGHEST


def top_structure(count):
    levels = count.bit_length()
    index = jnp.arange(count, dtype=jnp.int32)
    span = jnp.ones((count,), jnp.int32)
    for place in range(levels):
        span = span + ((index + 1) % (2 ** (place + 1)) == 0).astype(jnp.int32) * (2 ** place)
    row_index = index[:, None]
    col_index = index[None, :]
    keep = (col_index < row_index) & (col_index >= row_index + 1 - span[:, None])
    return keep.astype(jnp.float32)


def leaf_forward(top_total, rhs_part, blocks, inverses, struct):
    leaf_total = rhs_part.shape[0]
    updates = jnp.zeros((leaf_total + top_total,) + rhs_part.shape[1:], jnp.float32)
    values = jnp.zeros(rhs_part.shape, jnp.float32)

    def advance(position, state_pair):
        updates, values = state_pair
        source = lax.dynamic_index_in_dim(rhs_part, position, 0, False) - lax.dynamic_index_in_dim(updates, position, 0, False)
        solved = jnp.einsum("ck,ik->ci", source, lax.dynamic_index_in_dim(inverses, position, 0, False), precision=highest)
        targets = lax.dynamic_index_in_dim(struct, position, 0, False)
        outgoing = jnp.einsum("ck,rik->rci", solved, lax.dynamic_index_in_dim(blocks, position, 0, False), precision=highest)
        updates = updates.at[targets].add(outgoing)
        values = lax.dynamic_update_index_in_dim(values, solved, position, 0)
        return updates, values

    updates, values = lax.fori_loop(0, leaf_total, advance, (updates, values))
    return values, updates[leaf_total:]


def leaf_backward(forward_values, blocks, inverses, struct, top_values):
    leaf_total = forward_values.shape[0]
    solution_buffer = jnp.concatenate([jnp.zeros_like(forward_values), top_values], axis=0)

    def retreat(offset, solution_buffer):
        position = leaf_total - 1 - offset
        targets = lax.dynamic_index_in_dim(struct, position, 0, False)
        ancestors = jnp.take(solution_buffer, targets, axis=0)
        summed = jnp.einsum("rci,rik->ck", ancestors, lax.dynamic_index_in_dim(blocks, position, 0, False), precision=highest)
        own_rhs = lax.dynamic_index_in_dim(forward_values, position, 0, False)
        solved = jnp.einsum("ci,ik->ck", own_rhs - summed, lax.dynamic_index_in_dim(inverses, position, 0, False), precision=highest)
        return lax.dynamic_update_index_in_dim(solution_buffer, solved, position, 0)

    solution_buffer = lax.fori_loop(0, leaf_total, retreat, solution_buffer)
    return solution_buffer[:leaf_total]


def reference(rhs_leaf, rhs_top, leaf_blocks, leaf_dinv, leaf_struct, top_blocks, top_dinv):
    def shaped(array):
        return array.reshape((TOPS, LEAF) + array.shape[1:])

    keep = top_structure(TOPS)
    forward_leaf, leaf_updates = jax.vmap(partial(leaf_forward, TOPS))(shaped(rhs_leaf), shaped(leaf_blocks), shaped(leaf_dinv), shaped(leaf_struct))
    top_source = rhs_top - jnp.sum(leaf_updates, axis=0)

    def forward_turn(turn, buffer):
        keep_row = lax.dynamic_index_in_dim(keep, turn, 0, False)
        block_row = lax.dynamic_index_in_dim(top_blocks, turn, 0, False) * keep_row[:, None, None]
        pulled = jnp.einsum("jck,jik->ci", buffer, block_row, precision=highest)
        source = lax.dynamic_index_in_dim(top_source, turn, 0, False) - pulled
        solved = jnp.einsum("ck,ik->ci", source, lax.dynamic_index_in_dim(top_dinv, turn, 0, False), precision=highest)
        return lax.dynamic_update_index_in_dim(buffer, solved, turn, 0)

    forward_top = lax.fori_loop(0, TOPS, forward_turn, jnp.zeros(rhs_top.shape, jnp.float32))

    def backward_turn(offset, buffer):
        turn = TOPS - 1 - offset
        keep_col = lax.dynamic_index_in_dim(keep, turn, 1, False)
        block_col = lax.dynamic_index_in_dim(top_blocks, turn, 1, False) * keep_col[:, None, None]
        pushed = jnp.einsum("jci,jik->ck", buffer, block_col, precision=highest)
        source = lax.dynamic_index_in_dim(forward_top, turn, 0, False) - pushed
        solved = jnp.einsum("ci,ik->ck", source, lax.dynamic_index_in_dim(top_dinv, turn, 0, False), precision=highest)
        return lax.dynamic_update_index_in_dim(buffer, solved, turn, 0)

    top_solution = lax.fori_loop(0, TOPS, backward_turn, jnp.zeros(rhs_top.shape, jnp.float32))
    leaf_solution = jax.vmap(leaf_backward, in_axes=(0, 0, 0, 0, None))(forward_leaf, shaped(leaf_blocks), shaped(leaf_dinv), shaped(leaf_struct), top_solution)
    return leaf_solution.reshape(rhs_leaf.shape), top_solution
```

```python
import functools

import jax
import jax.numpy as jnp
from jax import lax
from jax.experimental import pallas as pl
from jax.experimental.pallas import tpu as pltpu
from jax.sharding import PartitionSpec as P

MESH = pl.DeviceIdType.MESH
f32 = jnp.float32
bf16 = jnp.bfloat16

CHUNK = 2
AHEAD = 2
TOP_Z, TOP_GROUP, TOP_SOLVER = 3, 6, 10


def split(x):
    high = x.astype(bf16)
    return high, (x - high.astype(f32)).astype(bf16)


def dot3(x, w, transposed):
    dims = (((1,), (1 if transposed else 0,)), ((), ()))
    dot = functools.partial(lax.dot_general, dimension_numbers=dims, preferred_element_type=f32)
    x_high, x_low = split(x)
    w_high, w_low = split(w)
    return dot(x_high, w_high) + (dot(x_high, w_low) + dot(x_low, w_high))


def trailing(q):
    count = 0
    while (q >> count) & 1:
        count += 1
    return count


def kernel(
    slot_ref, rl, rt, lb, ld, tb, td,
    o_leaf, o_top,
    acc, blk, dinv, fwd, zbuf, tg, rtop, part, contrib, gathered, upper, xs, xpath, zown, ftop,
    s_direct, s_relay, r_direct, r_relay,
    s_top, r_top, s_rt, r_rt, s_grp, r_grp, s_up, r_up, s_part, r_part, s_con, r_con, s_x, r_x, s_z, r_z,
    l_sem,
):
    leaf, cols, w = rl.shape
    quarter = w // 4
    half = quarter // 2
    cc = cols // 4
    chunks = leaf // CHUNK
    sn, z = lax.axis_index("sn"), lax.axis_index("rhs")
    g, c = sn // 4, sn % 4
    zr, zl, zo = lax.rem(z + 1, 4), lax.rem(z + 3, 4), lax.rem(z + 2, 4)
    solver = 2 * c
    is_solver = g == solver
    my_cols = pl.ds(pl.multiple_of(c * cc, cc), cc)

    def mate(i):
        return 4 * g + lax.rem(c + i, 4)

    def classmate(i):
        return 4 * lax.rem(g + i, 8) + c

    def remote(src, dst, ssem, rsem, device):
        return pltpu.make_async_remote_copy(
            src_ref=src, dst_ref=dst, send_sem=ssem, recv_sem=rsem, device_id=device, device_id_type=MESH
        )

    barrier = pltpu.get_barrier_semaphore()
    for i in range(1, 4):
        pl.semaphore_signal(barrier, inc=1, device_id=(sn, lax.rem(z + i, 4)), device_id_type=MESH)
        pl.semaphore_signal(barrier, inc=1, device_id=(mate(i), z), device_id_type=MESH)
    for i in range(1, 8):
        pl.semaphore_signal(barrier, inc=1, device_id=(classmate(i), z), device_id_type=MESH)

    locals_ = [
        pltpu.make_async_copy(rl, acc.at[pl.ds(0, leaf)], l_sem.at[0]),
        pltpu.make_async_copy(lb, blk.at[:, :, z], l_sem.at[1]),
        pltpu.make_async_copy(ld, dinv.at[:, z], l_sem.at[2]),
        pltpu.make_async_copy(td.at[0], tg.at[c, 0, z], l_sem.at[3]),
        pltpu.make_async_copy(rt.at[0, my_cols], rtop.at[c], l_sem.at[4]),
    ]
    ancestors = [(sn >> l) * (1 << l) + ((1 << l) - 1) for l in range(6)]
    for l in range(1, 6):
        locals_.append(pltpu.make_async_copy(tb.at[ancestors[l], 0], tg.at[c, l, z], l_sem.at[4 + l]))
    for copy in locals_:
        copy.start()
    acc[leaf:] = jnp.zeros((6, cols, w), f32)

    pl.semaphore_wait(barrier, 13)

    def direct(j, way):
        there = (sn, zr if way == 0 else zl)
        at = pl.ds(j * CHUNK, CHUNK)
        return [
            remote(lb.at[at], blk.at[at, :, z], s_direct.at[way, 0], r_direct.at[way, 0, j], there),
            remote(ld.at[at], dinv.at[at, z], s_direct.at[way, 1], r_direct.at[way, 1, j], there),
        ]

    def relay(j, way):
        there = (sn, zr if way == 0 else zl)
        owner = zl if way == 0 else zr
        at = pl.ds(j * CHUNK, CHUNK)
        rows = pl.ds(0 if way == 0 else half, half)
        b, d = blk.at[at, :, owner, rows], dinv.at[at, owner, rows]
        return [
            remote(b, b, s_relay.at[way, 0], r_relay.at[way, 0, j], there),
            remote(d, d, s_relay.at[way, 1], r_relay.at[way, 1, j], there),
        ]

    def direct_start(j):
        for way in range(2):
            for copy in direct(j, way):
                copy.start()

    direct_start(0)

    def top_z(i):
        there = (sn, lax.rem(z + i, 4))
        copies = [remote(td.at[0], tg.at[c, 0, z], s_top.at[i], r_top.at[i], there)]
        for l in range(1, 6):
            copies.append(remote(tb.at[ancestors[l], 0], tg.at[c, l, z], s_top.at[i], r_top.at[i], there))
        return copies

    def top_z_all(i):
        src = lax.rem(z + 4 - i, 4)
        view = tg.at[c, :, src]
        return remote(view, view, s_top.at[i], r_top.at[i], (sn, lax.rem(z + i, 4)))

    for i in range(1, 4):
        for copy in top_z(i):
            copy.start()

    def share_rhs(i):
        to = lax.rem(c + i, 4)
        return remote(
            rt.at[0, pl.ds(pl.multiple_of(to * cc, cc), cc)], rtop.at[c], s_rt.at[i], r_rt.at[i], (mate(i), z)
        )

    for i in range(1, 4):
        share_rhs(i).start()
    for j in range(1, AHEAD):
        direct_start(j)

    def share_group(i):
        return remote(tg.at[c], tg.at[c], s_grp.at[i], r_grp.at[i], (mate(i), z))

    def share_upper():
        there = (4 * solver + c, z)
        return [
            remote(tg.at[3, 0], upper.at[g, 0], s_up, r_up.at[g], there),
            remote(tg.at[3, pl.ds(3, 3)], upper.at[g, pl.ds(1, 3)], s_up, r_up.at[g], there),
        ]

    def upper_all(at):
        return remote(upper.at[at], upper.at[at], s_up, r_up.at[at], (4 * solver + c, z))

    for copy in locals_:
        copy.wait()

    def leaf_block(s):
        return blk[s].reshape(3 * w, w), dinv[s].reshape(w, w)

    def forward_step(s):
        b, d = leaf_block(s)
        solved = dot3(acc[s], d, True)
        fwd[s] = solved
        out = dot3(solved, b, True)
        acc[s + 1] = acc[s + 1] - out[:, :w]
        first, second = slot_ref[s, 1], slot_ref[s, 2]
        out1, out2 = out[:, w : 2 * w], out[:, 2 * w :]

        def push(t):
            m1 = (first == t).astype(f32)
            m2 = (second == t).astype(f32)
            acc[t] = acc[t] - (m1 * out1 + m2 * out2)

        for t in range(2, leaf + 6):
            push(t)

    def turn(j, carry):
        @pl.when(j + AHEAD < chunks)
        def _():
            direct_start(j + AHEAD)

        @pl.when(j < chunks)
        def _():
            for way in range(2):
                for copy in direct(j, way):
                    copy.wait_recv()
                for copy in relay(j, way):
                    copy.start()

        @pl.when(j == min(TOP_Z, chunks))
        def _():
            for i in range(1, 4):
                top_z_all(i).wait_recv()
            for i in range(1, 4):
                share_group(i).start()

        @pl.when(j == min(TOP_GROUP, chunks))
        def _():
            for i in range(1, 4):
                share_group(i).wait_recv()

            @pl.when(jnp.logical_not(is_solver))
            def _():
                for copy in share_upper():
                    copy.start()

        @pl.when(j >= 1)
        def _():
            for way in range(2):
                for copy in relay(j - 1, way):
                    copy.wait_recv()
            for i in range(CHUNK):
                forward_step((j - 1) * CHUNK + i)

        return carry

    lax.fori_loop(0, chunks + 1, turn, 0)

    def share_part(i):
        to = lax.rem(c + i, 4)
        return remote(
            acc.at[pl.ds(leaf, 6), pl.ds(pl.multiple_of(to * cc, cc), cc)],
            part.at[c],
            s_part.at[i],
            r_part.at[i],
            (mate(i), z),
        )

    for i in range(1, 4):
        share_part(i).start()
    part[c] = acc[pl.ds(leaf, 6), my_cols]

    for i in range(1, 4):
        share_rhs(i).wait_recv()
        share_part(i).wait_recv()

    def top_block(m, l):
        return tg[m, l].reshape(w, w)

    def top_stack(m):
        return tg[m, 2:6].reshape(4 * w, w)

    path = part[0] + part[1] + part[2] + part[3]
    f0 = dot3(path[0] + rtop[0], top_block(0, 0), True)
    f1 = dot3(path[1] + rtop[1] - dot3(f0, top_block(0, 1), True), top_block(1, 0), True)
    f2 = dot3(rtop[2], top_block(2, 0), True)
    out = dot3(f0, top_stack(0), True) + dot3(f1, top_stack(1), True) + dot3(f2, top_stack(2), True)
    ftop[0], ftop[1], ftop[2] = f0, f1, f2
    last = 4 * g + 3
    above = [(last + 1) % (1 << l) == 0 for l in range(6)] + [last + 1 == 64]
    for l in range(2, 6):
        mine = above[l]
        if l < 5:
            mine = jnp.logical_and(mine, jnp.logical_not(above[l + 1]))
        contrib[l - 2] = path[l] + mine.astype(f32) * rtop[3] - out[:, (l - 2) * w : (l - 1) * w]

    def share_contrib():
        return remote(contrib, gathered.at[g], s_con, r_con.at[g], (4 * solver + c, z))

    def contrib_from(at):
        return remote(gathered.at[at], gathered.at[at], s_con, r_con.at[at], (4 * solver + c, z))

    def share_x(i):
        to = lax.rem(g + i, 8)
        return remote(xs.at[to], xpath, s_x.at[i], r_x, (classmate(i), z))

    @pl.when(jnp.logical_not(is_solver))
    def _():
        share_contrib().start()

    @pl.when(is_solver)
    def _():
        upper[g, 0] = tg[3, 0]
        upper[g, 1:4] = tg[3, 3:6]
        gathered[g] = contrib[...]
        for i in range(1, 8):
            at = lax.rem(g + i, 8)
            upper_all(at).wait_recv()
            contrib_from(at).wait_recv()

        def upper_block(q, slot):
            return upper[q, slot].reshape(w, w)

        spans = [range(q + 1 - (1 << trailing(q)), q) for q in range(8)]
        order = sorted(range(8), key=lambda q: (trailing(q), q))
        forward = {}
        for q in order:
            level = trailing(q)
            source = gathered[q, level]
            for below in spans[q]:
                source = source + gathered[below, level]
            for below in spans[q]:
                source = source - dot3(forward[below], upper_block(below, level), True)
            forward[q] = dot3(source, upper_block(q, 0), True)
        solved = {}
        for q in reversed(order):
            source = forward[q]
            for up in range(q + 1, 8):
                if q in spans[up]:
                    source = source - dot3(solved[up], upper_block(q, trailing(up)), False)
            solved[q] = dot3(source, upper_block(q, 0), False)
        for to in range(8):
            for level in range(4):
                q = (to >> level) * (1 << level) + (1 << level) - 1
                if trailing(q) == level:
                    xs[to, level] = solved[q]
                else:
                    xs[to, level] = jnp.zeros((cc, w), f32)
        for i in range(1, 8):
            share_x(i).start()
        xpath[...] = xs[g]

    @pl.when(jnp.logical_not(is_solver))
    def _():
        remote(xpath, xpath, s_x.at[0], r_x, (4 * solver + c, z)).wait_recv()

    across = jnp.concatenate([xpath[0], xpath[1], xpath[2], xpath[3]], axis=1)
    x1 = dot3(ftop[1] - dot3(across, top_stack(1), False), top_block(1, 0), False)
    x2 = dot3(ftop[2] - dot3(across, top_stack(2), False), top_block(2, 0), False)
    x0 = dot3(
        ftop[0] - dot3(across, top_stack(0), False) - dot3(x1, top_block(0, 1), False), top_block(0, 0), False
    )
    zown[0], zown[1], zown[6] = x0, x1, x2
    zown[2:6] = xpath[...]

    def share_z(i):
        return remote(zown, zbuf.at[pl.ds(leaf, 7), my_cols], s_z.at[i], r_z.at[i], (mate(i), z))

    def z_from(i):
        src = lax.rem(c + 4 - i, 4)
        view = zbuf.at[pl.ds(leaf, 7), pl.ds(pl.multiple_of(src * cc, cc), cc)]
        return remote(zown, view, s_z.at[i], r_z.at[i], (mate(i), z))

    for i in range(1, 4):
        share_z(i).start()
    zbuf[pl.ds(leaf, 7), my_cols] = zown[...]
    for i in range(1, 4):
        z_from(i).wait_recv()

    def backward(offset, carry):
        s = leaf - 1 - offset
        b, d = leaf_block(s)
        z_at = jnp.concatenate([zbuf[s + 1], zbuf[slot_ref[s, 1]], zbuf[slot_ref[s, 2]]], axis=1)
        zbuf[s] = dot3(fwd[s] - dot3(z_at, b, False), d, False)
        return carry

    lax.fori_loop(0, leaf, backward, 0)

    level = sum(jnp.where((sn + 1) % (1 << l) == 0, 1, 0) for l in range(1, 6))
    place = jnp.where(c == 2, 6, level)
    outs = [
        pltpu.make_async_copy(zbuf.at[pl.ds(0, leaf)], o_leaf, l_sem.at[0]),
        pltpu.make_async_copy(zbuf.at[leaf + place], o_top.at[0], l_sem.at[1]),
    ]
    for copy in outs:
        copy.start()

    whole = pl.ds(0, leaf)
    for way in range(2):
        there = (sn, zr if way == 0 else zl)
        owner = zl if way == 0 else zr
        rows = pl.ds(0 if way == 0 else half, half)
        remote(lb, blk.at[:, :, z], s_direct.at[way, 0], r_direct.at[way, 0, 0], there).wait_send()
        remote(ld, dinv.at[:, z], s_direct.at[way, 1], r_direct.at[way, 1, 0], there).wait_send()
        b, d = blk.at[whole, :, owner, rows], dinv.at[whole, owner, rows]
        remote(b, b, s_relay.at[way, 0], r_relay.at[way, 0, 0], there).wait_send()
        remote(d, d, s_relay.at[way, 1], r_relay.at[way, 1, 0], there).wait_send()
    for i in range(1, 4):
        top_z_all(i).wait_send()
        share_rhs(i).wait_send()
        share_group(i).wait_send()
        share_part(i).wait_send()
        share_z(i).wait_send()

    @pl.when(jnp.logical_not(is_solver))
    def _():
        upper_all(g).wait_send()
        share_contrib().wait_send()

    @pl.when(is_solver)
    def _():
        for i in range(1, 8):
            share_x(i).wait_send()

    for copy in outs:
        copy.wait()


def call(rl, rt, lb, ld, slots, tb, td):
    leaf, cols, w = rl.shape
    cc, quarter, chunks = cols // 4, w // 4, leaf // CHUNK
    any_spec = pl.BlockSpec(memory_space=pl.ANY)
    dma = pltpu.SemaphoreType.DMA
    return pl.pallas_call(
        kernel,
        out_shape=(jax.ShapeDtypeStruct(rl.shape, f32), jax.ShapeDtypeStruct(rt.shape, f32)),
        in_specs=[pl.BlockSpec(memory_space=pltpu.SMEM)] + [any_spec] * 6,
        out_specs=(any_spec, any_spec),
        scratch_shapes=[
            pltpu.VMEM((leaf + 6, cols, w), f32),
            pltpu.VMEM((leaf, 3, 4, quarter, w), f32),
            pltpu.VMEM((leaf, 4, quarter, w), f32),
            pltpu.VMEM((leaf, cols, w), f32),
            pltpu.VMEM((leaf + 7, cols, w), f32),
            pltpu.VMEM((4, 6, 4, quarter, w), f32),
            pltpu.VMEM((4, cc, w), f32),
            pltpu.VMEM((4, 6, cc, w), f32),
            pltpu.VMEM((4, cc, w), f32),
            pltpu.VMEM((8, 4, cc, w), f32),
            pltpu.VMEM((8, 4, 4, quarter, w), f32),
            pltpu.VMEM((8, 4, cc, w), f32),
            pltpu.VMEM((4, cc, w), f32),
            pltpu.VMEM((7, cc, w), f32),
            pltpu.VMEM((3, cc, w), f32),
            dma((2, 2)), dma((2, 2)), dma((2, 2, chunks)), dma((2, 2, chunks)),
            dma((4,)), dma((4,)), dma((4,)), dma((4,)), dma((4,)), dma((4,)),
            dma, dma((8,)), dma((4,)), dma((4,)), dma, dma((8,)), dma((8,)), dma, dma((4,)), dma((4,)),
            dma((10,)),
        ],
        compiler_params=pltpu.CompilerParams(
            collective_id=0, has_side_effects=True, vmem_limit_bytes=60 * 1024 * 1024
        ),
        name="substitution",
    )(slots, rl, rt, lb, ld, tb, td)


def local(rhs_leaf, rhs_top, leaf_blocks, leaf_dinv, leaf_struct, top_blocks, top_dinv):
    leaf = rhs_leaf.shape[0]
    top = leaf_struct - leaf
    level = sum(((top + 1) % (1 << l) == 0).astype(jnp.int32) for l in range(1, 6))
    slots = jnp.where(top < 0, leaf_struct, leaf + level)
    return call(rhs_leaf, rhs_top, leaf_blocks, leaf_dinv, slots, top_blocks, top_dinv)


def solution(mesh):
    return jax.shard_map(
        local,
        mesh=mesh,
        in_specs=(
            P("sn", "rhs", None),
            P("sn", "rhs", None),
            P("sn", None, "rhs", None),
            P("sn", "rhs", None),
            P("sn", None),
            P(None, "sn", "rhs", None),
            P("sn", "rhs", None),
        ),
        out_specs=(P("sn", "rhs", None), P("sn", "rhs", None)),
        check_vma=False,
    )
```

```python
import functools

import jax
import jax.numpy as jnp
from jax import lax
from jax.experimental import pallas as pl
from jax.experimental.pallas import tpu as pltpu
from jax.sharding import PartitionSpec as P

MESH = pl.DeviceIdType.MESH
f32 = jnp.float32
bf16 = jnp.bfloat16

CHUNK = 2
AHEAD = 2
TOP_Z, TOP_GROUP, TOP_SOLVER = 3, 6, 10


def split(x):
    high = x.astype(bf16)
    return high, (x - high.astype(f32)).astype(bf16)


def dot3(x, w, transposed):
    dims = (((1,), (1 if transposed else 0,)), ((), ()))
    dot = functools.partial(lax.dot_general, dimension_numbers=dims, preferred_element_type=f32)
    x_high, x_low = split(x)
    w_high, w_low = split(w)
    return dot(x_high, w_high) + (dot(x_high, w_low) + dot(x_low, w_high))


def trailing(q):
    count = 0
    while (q >> count) & 1:
        count += 1
    return count


def kernel(
    st, rl, rt, lb, ld, tb, td,
    o_leaf, o_top,
    acc, rin, blk, dinv, fwd, zbuf, tg, rtop, part, contrib, gathered, upper, xs, xpath, zown, ftop, tout, stv, slot_ref,
    s_own, s_fwd, s_rhs, s_back, r_in, r_rhs, r_back,
    s_top, r_top, s_rt, r_rt, s_grp, r_grp, s_up, r_up, s_part, r_part, s_con, r_con, s_x, r_x, s_z, r_z, s_to, r_to,
    s_st, r_st, l_sem,
):
    leaf, cols, w = rl.shape
    quarter = w // 4
    cc = cols // 4
    chunks = leaf // CHUNK
    sn, z = lax.axis_index("sn"), lax.axis_index("rhs")
    g, c = sn // 4, sn % 4
    core, low = sn % 2, z // 2
    hub = core == low
    guest = jnp.logical_not(hub)
    role = jnp.where(hub, 0, 1)
    other, zm, zo = sn + 1 - 2 * core, z + 1 - 2 * (z % 2), 3 - z
    rows_of = (z, zo, zm, 3 - zm)
    place = 2 * (c // 2) + role
    solver = 2 * c
    is_solver = g == solver
    block = jnp.where(hub, z, zo)

    def at_cols(k):
        return pl.ds(pl.multiple_of(k * cc, cc), cc)

    my_cols = at_cols(place)

    def sibling(i):
        return 4 * g + lax.rem(c + i, 4)

    def classmate(i):
        return 4 * lax.rem(g + i, 8) + c

    def mate(k, i):
        to = lax.rem(k + i, 4)
        return to, (4 * g + 2 * (to // 2) + core, jnp.where(to % 2 == role, z, zo))

    def worker(k):
        return 4 * g + 2 * (k // 2) + low, (z if k % 2 == 0 else zo)

    def remote(src, dst, ssem, rsem, device):
        return pltpu.make_async_remote_copy(
            src_ref=src, dst_ref=dst, send_sem=ssem, recv_sem=rsem, device_id=device, device_id_type=MESH
        )

    barrier = pltpu.get_barrier_semaphore()

    def greet(device):
        pl.semaphore_signal(barrier, inc=1, device_id=device, device_id_type=MESH)

    for i in range(1, 4):
        greet((sibling(i), z))
    for i in range(4):
        greet((sibling(i), zo))
    greet((sn, zm))
    greet((sn, 3 - zm))
    for i in range(1, 8):
        greet((classmate(i), z))

    locals_ = [pltpu.make_async_copy(td.at[0], tg.at[c, 0, z], l_sem.at[0])]
    ancestors = [(sn >> l) * (1 << l) + ((1 << l) - 1) for l in range(6)]
    for l in range(1, 6):
        locals_.append(pltpu.make_async_copy(tb.at[ancestors[l], 0], tg.at[c, l, z], l_sem.at[l]))
    hub_locals = [
        pltpu.make_async_copy(rl, rin, l_sem.at[6]),
        pltpu.make_async_copy(lb, blk.at[:, :, z], l_sem.at[7]),
        pltpu.make_async_copy(ld, dinv.at[:, z], l_sem.at[8]),
        pltpu.make_async_copy(st, stv, l_sem.at[9]),
        pltpu.make_async_copy(rt.at[0, my_cols], rtop.at[c], l_sem.at[10]),
    ]
    for copy in locals_:
        copy.start()

    @pl.when(hub)
    def _():
        for copy in hub_locals:
            copy.start()

    def clear(t, carry):
        acc[t] = jnp.zeros((cols, w), f32)
        return carry

    lax.fori_loop(0, leaf + 6, clear, 0)
    pl.semaphore_wait(barrier, 16)

    def piece(j, k):
        at = pl.ds(j * CHUNK, CHUNK)
        return blk.at[at, :, rows_of[k]], dinv.at[at, rows_of[k]]

    def own(j, to, k, device):
        at = pl.ds(j * CHUNK, CHUNK)
        return [
            remote(lb.at[at], blk.at[at, :, z], s_own.at[to, 0], r_in.at[k, 0, j], device),
            remote(ld.at[at], dinv.at[at, z], s_own.at[to, 1], r_in.at[k, 1, j], device),
        ]

    def onward(j, k, to, into, device):
        b, d = piece(j, k)
        return [
            remote(b, b, s_fwd.at[to, 0], r_in.at[into, 0, j], device),
            remote(d, d, s_fwd.at[to, 1], r_in.at[into, 1, j], device),
        ]

    def arrived(j, k):
        for copy in onward(j, k, 0, k, (sn, zm)):
            copy.wait_recv()

    def rhs_piece(j):
        at = pl.ds(j * CHUNK, CHUNK)
        return remote(rl.at[at], rin.at[at], s_rhs, r_rhs.at[j], (other, zo))

    def send_own(j):
        @pl.when(hub)
        def _():
            for copy in own(j, 0, 2, (sn, zm)) + own(j, 1, 0, (other, z)):
                copy.start()

        @pl.when(guest)
        def _():
            rhs_piece(j).start()
            for copy in own(j, 0, 1, (sn, zo)):
                copy.start()

    send_own(0)
    to_guest = remote(st, stv, s_st, r_st, (other, z))

    @pl.when(hub)
    def _():
        to_guest.start()

    def share_rhs(k):
        return remote(rt.at[0, at_cols(k)], rtop.at[c], s_rt.at[k], r_rt.at[c], worker(k))

    def rhs_from(m):
        return remote(rtop.at[m], rtop.at[m], s_rt.at[0], r_rt.at[m], (4 * g + m, zo))

    def not_me(k):
        return jnp.logical_or(guest, place != k)

    def not_own(m):
        return jnp.logical_or(guest, c != m)

    for k in range(4):

        @pl.when(not_me(k))
        def _(k=k):
            share_rhs(k).start()

    for j in range(1, AHEAD):
        send_own(j)

    def top_z(i):
        there = (sn, lax.rem(z + i, 4))
        copies = [remote(td.at[0], tg.at[c, 0, z], s_top.at[i], r_top.at[i], there)]
        for l in range(1, 6):
            copies.append(remote(tb.at[ancestors[l], 0], tg.at[c, l, z], s_top.at[i], r_top.at[i], there))
        return copies

    def top_z_all(i):
        src = lax.rem(z + 4 - i, 4)
        view = tg.at[c, :, src]
        return remote(view, view, s_top.at[i], r_top.at[i], (sn, lax.rem(z + i, 4)))

    for i in range(1, 4):
        for copy in top_z(i):
            copy.start()

    def share_group(i):
        return remote(tg.at[c], tg.at[c], s_grp.at[i], r_grp.at[i], (sibling(i), z))

    def share_upper():
        there = (4 * solver + c, z)
        return [
            remote(tg.at[3, 0], upper.at[g, 0], s_up, r_up.at[g], there),
            remote(tg.at[3, pl.ds(3, 3)], upper.at[g, pl.ds(1, 3)], s_up, r_up.at[g], there),
        ]

    def upper_all(at):
        return remote(upper.at[at], upper.at[at], s_up, r_up.at[at], (4 * solver + c, z))

    for copy in locals_:
        copy.wait()

    @pl.when(hub)
    def _():
        for copy in hub_locals:
            copy.wait()

    @pl.when(guest)
    def _():
        to_guest.wait_recv()

    into_smem = pltpu.make_async_copy(stv, slot_ref, l_sem.at[11])
    into_smem.start()
    into_smem.wait()

    def slot_of(s, r):
        v = slot_ref[s, r]
        t = v - (leaf - 1)
        level = 0
        for l in range(1, 6):
            level = level + jnp.where((t & ((1 << l) - 1)) == 0, 1, 0)
        return jnp.where(v < leaf, v, leaf + level)

    def leaf_block(s):
        return blk[s].reshape(3 * w, w), dinv[s].reshape(w, w)

    def forward_step(s):
        b, d = leaf_block(s)
        solved = dot3(rin[s] + acc[s], d, True)
        fwd[s] = solved
        out = dot3(solved, b, True)
        acc[s + 1] = acc[s + 1] - out[:, :w]
        first, second = slot_of(s, 1), slot_of(s, 2)
        out1, out2 = out[:, w : 2 * w], out[:, 2 * w :]

        def push(t):
            m1 = (first == t).astype(f32)
            m2 = (second == t).astype(f32)
            acc[t] = acc[t] - (m1 * out1 + m2 * out2)

        for t in range(2, leaf + 6):
            push(t)

    def turn(j, carry):
        @pl.when(j + AHEAD < chunks)
        def _():
            send_own(j + AHEAD)

        @pl.when(hub)
        def _():
            @pl.when(j < chunks)
            def _():
                arrived(j, 1)
                for copy in onward(j, 1, 0, 3, (sn, zm)) + onward(j, 1, 1, 1, (other, z)):
                    copy.start()
                arrived(j, 2)
                for copy in onward(j, 2, 2, 2, (other, z)):
                    copy.start()

            @pl.when(j >= 1)
            def _():
                arrived(j - 1, 3)
                for copy in onward(j - 1, 3, 3, 3, (other, z)):
                    copy.start()

        @pl.when(j == min(TOP_Z, chunks))
        def _():
            for i in range(1, 4):
                top_z_all(i).wait_recv()
            for i in range(1, 4):
                share_group(i).start()

        @pl.when(j == min(TOP_GROUP, chunks))
        def _():
            for i in range(1, 4):
                share_group(i).wait_recv()

            @pl.when(jnp.logical_not(is_solver))
            def _():
                for copy in share_upper():
                    copy.start()

        @pl.when(j >= 1)
        def _():
            @pl.when(guest)
            def _():
                rhs_piece(j - 1).wait_recv()
                for k in range(4):
                    arrived(j - 1, k)

            for i in range(CHUNK):
                forward_step((j - 1) * CHUNK + i)

        return carry

    lax.fori_loop(0, chunks + 1, turn, 0)

    def share_part(i):
        to, device = mate(place, i)
        return remote(acc.at[pl.ds(leaf, 6), at_cols(to)], part.at[place], s_part.at[i], r_part.at[i], device)

    for i in range(1, 4):
        share_part(i).start()
    part[place] = acc[pl.ds(leaf, 6), my_cols]

    for m in range(4):

        @pl.when(not_own(m))
        def _(m=m):
            rhs_from(m).wait_recv()

    for i in range(1, 4):
        share_part(i).wait_recv()

    def top_block(m, l):
        return tg[m, l].reshape(w, w)

    def top_stack(m):
        return tg[m, 2:6].reshape(4 * w, w)

    path = part[0] + part[1] + part[2] + part[3]
    f0 = dot3(path[0] + rtop[0], top_block(0, 0), True)
    f1 = dot3(path[1] + rtop[1] - dot3(f0, top_block(0, 1), True), top_block(1, 0), True)
    f2 = dot3(rtop[2], top_block(2, 0), True)
    out = dot3(f0, top_stack(0), True) + dot3(f1, top_stack(1), True) + dot3(f2, top_stack(2), True)
    ftop[0], ftop[1], ftop[2] = f0, f1, f2
    last = 4 * g + 3
    above = [(last + 1) % (1 << l) == 0 for l in range(6)]
    for l in range(2, 6):
        mine = above[l]
        if l < 5:
            mine = jnp.logical_and(mine, jnp.logical_not(above[l + 1]))
        contrib[l - 2] = path[l] + mine.astype(f32) * rtop[3] - out[:, (l - 2) * w : (l - 1) * w]

    def share_contrib():
        return remote(contrib, gathered.at[g], s_con, r_con.at[g], (4 * solver + c, z))

    def contrib_from(at):
        return remote(gathered.at[at], gathered.at[at], s_con, r_con.at[at], (4 * solver + c, z))

    def share_x(i):
        to = lax.rem(g + i, 8)
        return remote(xs.at[to], xpath, s_x.at[i], r_x, (classmate(i), z))

    @pl.when(jnp.logical_not(is_solver))
    def _():
        share_contrib().start()

    @pl.when(is_solver)
    def _():
        upper[g, 0] = tg[3, 0]
        upper[g, 1:4] = tg[3, 3:6]
        gathered[g] = contrib[...]
        for i in range(1, 8):
            at = lax.rem(g + i, 8)
            upper_all(at).wait_recv()
            contrib_from(at).wait_recv()

        def upper_block(q, slot):
            return upper[q, slot].reshape(w, w)

        spans = [range(q + 1 - (1 << trailing(q)), q) for q in range(8)]
        order = sorted(range(8), key=lambda q: (trailing(q), q))
        forward = {}
        for q in order:
            level = trailing(q)
            source = gathered[q, level]
            for below in spans[q]:
                source = source + gathered[below, level]
            for below in spans[q]:
                source = source - dot3(forward[below], upper_block(below, level), True)
            forward[q] = dot3(source, upper_block(q, 0), True)
        solved = {}
        for q in reversed(order):
            source = forward[q]
            for up in range(q + 1, 8):
                if q in spans[up]:
                    source = source - dot3(solved[up], upper_block(q, trailing(up)), False)
            solved[q] = dot3(source, upper_block(q, 0), False)
        for to in range(8):
            for level in range(4):
                q = (to >> level) * (1 << level) + (1 << level) - 1
                if trailing(q) == level:
                    xs[to, level] = solved[q]
                else:
                    xs[to, level] = jnp.zeros((cc, w), f32)
        for i in range(1, 8):
            share_x(i).start()
        xpath[...] = xs[g]

    @pl.when(jnp.logical_not(is_solver))
    def _():
        remote(xpath, xpath, s_x.at[0], r_x, (4 * solver + c, z)).wait_recv()

    across = jnp.concatenate([xpath[0], xpath[1], xpath[2], xpath[3]], axis=1)
    x1 = dot3(ftop[1] - dot3(across, top_stack(1), False), top_block(1, 0), False)
    x2 = dot3(ftop[2] - dot3(across, top_stack(2), False), top_block(2, 0), False)
    x0 = dot3(
        ftop[0] - dot3(across, top_stack(0), False) - dot3(x1, top_block(0, 1), False), top_block(0, 0), False
    )
    zown[0], zown[1], zown[6] = x0, x1, x2
    zown[2:6] = xpath[...]

    def share_z(i):
        to, device = mate(place, i)
        return remote(zown.at[pl.ds(0, 6)], zbuf.at[pl.ds(leaf, 6), my_cols], s_z.at[i], r_z.at[i], device)

    def z_from(i):
        view = zbuf.at[pl.ds(leaf, 6), at_cols(lax.rem(place + 4 - i, 4))]
        return remote(zown.at[pl.ds(0, 6)], view, s_z.at[i], r_z.at[i], mate(place, i)[1])

    for i in range(1, 4):
        share_z(i).start()
    zbuf[pl.ds(leaf, 6), my_cols] = zown[0:6]

    def level_of(t):
        return sum(jnp.where((t + 1) % (1 << l) == 0, 1, 0) for l in range(1, 6))

    top_slots = (0, 1, 6, level_of(last))

    def share_top(m):
        return remote(zown.at[top_slots[m]], tout.at[my_cols], s_to.at[m], r_to.at[place], (4 * g + m, block))

    def top_from(k):
        return remote(zown.at[0], tout.at[at_cols(k)], s_to.at[0], r_to.at[k], worker(k))

    for m in range(4):

        @pl.when(not_own(m))
        def _(m=m):
            share_top(m).start()

    @pl.when(hub)
    def _():
        tout[my_cols] = zown[jnp.where(c == 2, 6, level_of(sn))]

    for i in range(1, 4):
        z_from(i).wait_recv()

    def back_piece(j):
        at = pl.ds(leaf - (j + 1) * CHUNK, CHUNK)
        return remote(zbuf.at[at], o_leaf.at[at], s_back, r_back, (other, zo))

    def keep_piece(j):
        at = pl.ds(leaf - (j + 1) * CHUNK, CHUNK)
        return pltpu.make_async_copy(zbuf.at[at], o_leaf.at[at], l_sem.at[0])

    def let_go(j):
        @pl.when(hub)
        def _():
            keep_piece(j).start()

        @pl.when(guest)
        def _():
            back_piece(j).start()

    def backward(j, carry):
        for i in range(CHUNK):
            s = leaf - 1 - j * CHUNK - i
            b, d = leaf_block(s)
            z_at = jnp.concatenate([zbuf[s + 1], zbuf[slot_of(s, 1)], zbuf[slot_of(s, 2)]], axis=1)
            zbuf[s] = dot3(fwd[s] - dot3(z_at, b, False), d, False)

        @pl.when(j >= 1)
        def _():
            let_go(j - 1)

        return carry

    lax.fori_loop(0, chunks, backward, 0)

    for k in range(4):

        @pl.when(not_me(k))
        def _(k=k):
            top_from(k).wait_recv()

    top_out = pltpu.make_async_copy(tout, o_top.at[0], l_sem.at[1])
    top_out.start()
    let_go(chunks - 1)

    whole = pl.ds(0, leaf)

    def left(ssem, rows):
        b, d = blk.at[:, :, rows], dinv.at[:, rows]
        remote(b, b, ssem.at[0], r_in.at[0, 0, 0], (sn, zo)).wait_send()
        remote(d, d, ssem.at[1], r_in.at[0, 1, 0], (sn, zo)).wait_send()

    left(s_own.at[0], z)
    for i in range(1, 4):
        top_z_all(i).wait_send()
        share_group(i).wait_send()
        share_part(i).wait_send()
        share_z(i).wait_send()
    for m in range(4):

        @pl.when(not_me(m))
        def _(m=m):
            share_rhs(m).wait_send()

        @pl.when(not_own(m))
        def _(m=m):
            share_top(m).wait_send()

    @pl.when(jnp.logical_not(is_solver))
    def _():
        upper_all(g).wait_send()
        share_contrib().wait_send()

    @pl.when(is_solver)
    def _():
        for i in range(1, 8):
            share_x(i).wait_send()

    @pl.when(hub)
    def _():
        left(s_own.at[1], z)
        for to in range(4):
            left(s_fwd.at[to], z)
        to_guest.wait_send()
        pltpu.make_async_copy(zbuf.at[whole], o_leaf, l_sem.at[0]).wait()

    @pl.when(guest)
    def _():
        remote(rl, rin, s_rhs, r_rhs.at[0], (other, zo)).wait_send()
        everything = remote(zbuf.at[whole], o_leaf, s_back, r_back, (other, zo))
        everything.wait_send()
        everything.wait_recv()

    top_out.wait()


def local(rl, rt, lb, ld, st, tb, td):
    leaf, cols, w = rl.shape
    cc, quarter, chunks = cols // 4, w // 4, leaf // CHUNK
    any_spec = pl.BlockSpec(memory_space=pl.ANY)
    dma = pltpu.SemaphoreType.DMA
    return pl.pallas_call(
        kernel,
        out_shape=(jax.ShapeDtypeStruct(rl.shape, f32), jax.ShapeDtypeStruct(rt.shape, f32)),
        in_specs=[any_spec] * 7,
        out_specs=(any_spec, any_spec),
        scratch_shapes=[
            pltpu.VMEM((leaf + 6, cols, w), f32),
            pltpu.VMEM((leaf, cols, w), f32),
            pltpu.VMEM((leaf, 3, 4, quarter, w), f32),
            pltpu.VMEM((leaf, 4, quarter, w), f32),
            pltpu.VMEM((leaf, cols, w), f32),
            pltpu.VMEM((leaf + 6, cols, w), f32),
            pltpu.VMEM((4, 6, 4, quarter, w), f32),
            pltpu.VMEM((4, cc, w), f32),
            pltpu.VMEM((4, 6, cc, w), f32),
            pltpu.VMEM((4, cc, w), f32),
            pltpu.VMEM((8, 4, cc, w), f32),
            pltpu.VMEM((8, 4, 4, quarter, w), f32),
            pltpu.VMEM((8, 4, cc, w), f32),
            pltpu.VMEM((4, cc, w), f32),
            pltpu.VMEM((7, cc, w), f32),
            pltpu.VMEM((3, cc, w), f32),
            pltpu.VMEM((cols, w), f32),
            pltpu.VMEM(st.shape, jnp.int32),
            pltpu.SMEM(st.shape, jnp.int32),
            dma((2, 2)), dma((4, 2)), dma, dma, dma((4, 2, chunks)), dma((chunks,)), dma,
            dma((4,)), dma((4,)), dma((4,)), dma((4,)), dma((4,)), dma((4,)),
            dma, dma((8,)), dma((4,)), dma((4,)), dma, dma((8,)), dma((8,)), dma, dma((4,)), dma((4,)),
            dma((4,)), dma((4,)), dma, dma, dma((12,)),
        ],
        compiler_params=pltpu.CompilerParams(
            collective_id=0, has_side_effects=True, vmem_limit_bytes=60 * 1024 * 1024
        ),
        name="substitution",
    )(st, rl, rt, lb, ld, tb, td)


def solution(mesh):
    return jax.shard_map(
        local,
        mesh=mesh,
        in_specs=(
            P("sn", "rhs", None),
            P("sn", "rhs", None),
            P("sn", None, "rhs", None),
            P("sn", "rhs", None),
            P("sn", None),
            P(None, "sn", "rhs", None),
            P("sn", "rhs", None),
        ),
        out_specs=(P("sn", "rhs", None), P("sn", "rhs", None)),
        check_vma=False,
    )
```

```python
import functools

import jax
import jax.numpy as jnp
from jax import lax
from jax.experimental import pallas as pl
from jax.experimental.pallas import tpu as pltpu
from jax.sharding import PartitionSpec as P

MESH = pl.DeviceIdType.MESH
f32 = jnp.float32
bf16 = jnp.bfloat16

CHUNK = 2
AHEAD = 3
LAG = 2
TOP_Z, TOP_GROUP = 3, 11


def split(x):
    high = x.astype(bf16)
    return high, (x - high.astype(f32)).astype(bf16)


def dot3(x, w, transposed):
    dims = (((1,), (1 if transposed else 0,)), ((), ()))
    dot = functools.partial(lax.dot_general, dimension_numbers=dims, preferred_element_type=f32)
    x_high, x_low = split(x)
    w_high, w_low = split(w)
    return dot(x_high, w_high) + (dot(x_high, w_low) + dot(x_low, w_high))


def trailing(q):
    count = 0
    while (q >> count) & 1:
        count += 1
    return count


def kernel(
    st, rl, rt, lb, ld, tb, td,
    o_leaf, o_top,
    acc, rin, blk, dinv, fwd, zbuf, tg, rtop, part, contrib, gathered, upper, xs, xpath, zown, ftop, tout, stv, slot_ref,
    s_own, s_fwd, s_rhs, s_back, r_in, r_rhs, r_back,
    s_top, r_top, s_rt, r_rt, s_grp, r_grp, s_up, r_up, s_part, r_part, s_con, r_con, s_x, r_x, s_z, r_z, s_to, r_to,
    s_st, r_st, l_sem,
):
    leaf, cols, w = rl.shape
    quarter = w // 4
    cc = cols // 4
    chunks = leaf // CHUNK
    sn, z = lax.axis_index("sn"), lax.axis_index("rhs")
    g, c = sn // 4, sn % 4
    core, low = sn % 2, z // 2
    hub = core == low
    guest = jnp.logical_not(hub)
    role = jnp.where(hub, 0, 1)
    other, zm, zo = sn + 1 - 2 * core, z + 1 - 2 * (z % 2), 3 - z
    rows_of = (z, zo, zm, 3 - zm)
    place = 2 * (c // 2) + role
    solver = 2 * c
    is_solver = g == solver
    block = jnp.where(hub, z, zo)

    def at_cols(k):
        return pl.ds(pl.multiple_of(k * cc, cc), cc)

    my_cols = at_cols(place)

    def sibling(i):
        return 4 * g + lax.rem(c + i, 4)

    def classmate(i):
        return 4 * lax.rem(g + i, 8) + c

    def mate(k, i):
        to = lax.rem(k + i, 4)
        return to, (4 * g + 2 * (to // 2) + core, jnp.where(to % 2 == role, z, zo))

    def worker(k):
        return 4 * g + 2 * (k // 2) + low, (z if k % 2 == 0 else zo)

    def remote(src, dst, ssem, rsem, device):
        return pltpu.make_async_remote_copy(
            src_ref=src, dst_ref=dst, send_sem=ssem, recv_sem=rsem, device_id=device, device_id_type=MESH
        )

    barrier = pltpu.get_barrier_semaphore()

    def greet(device):
        pl.semaphore_signal(barrier, inc=1, device_id=device, device_id_type=MESH)

    for i in range(1, 4):
        greet((sibling(i), z))
    for i in range(4):
        greet((sibling(i), zo))
    greet((sn, zm))
    greet((sn, 3 - zm))
    for i in range(1, 8):
        greet((classmate(i), z))

    locals_ = [pltpu.make_async_copy(td.at[0], tg.at[c, 0, z], l_sem.at[0])]
    ancestors = [(sn >> l) * (1 << l) + ((1 << l) - 1) for l in range(6)]
    for l in range(1, 6):
        locals_.append(pltpu.make_async_copy(tb.at[ancestors[l], 0], tg.at[c, l, z], l_sem.at[l]))
    hub_locals = [
        pltpu.make_async_copy(rl, rin, l_sem.at[6]),
        pltpu.make_async_copy(lb, blk.at[:, :, z], l_sem.at[7]),
        pltpu.make_async_copy(ld, dinv.at[:, z], l_sem.at[8]),
        pltpu.make_async_copy(st, stv, l_sem.at[9]),
        pltpu.make_async_copy(rt.at[0, my_cols], rtop.at[c], l_sem.at[10]),
    ]
    for copy in locals_:
        copy.start()

    @pl.when(hub)
    def _():
        for copy in hub_locals:
            copy.start()

    def clear(t, carry):
        acc[t] = jnp.zeros((cols, w), f32)
        return carry

    lax.fori_loop(0, leaf + 6, clear, 0)
    pl.semaphore_wait(barrier, 16)

    def piece(j, k):
        at = pl.ds(j * CHUNK, CHUNK)
        return blk.at[at, :, rows_of[k]], dinv.at[at, rows_of[k]]

    def own(j, to, k, device):
        at = pl.ds(j * CHUNK, CHUNK)
        return [
            remote(lb.at[at], blk.at[at, :, z], s_own.at[to, 0], r_in.at[k, 0, j], device),
            remote(ld.at[at], dinv.at[at, z], s_own.at[to, 1], r_in.at[k, 1, j], device),
        ]

    def onward(j, k, to, into, device):
        b, d = piece(j, k)
        return [
            remote(b, b, s_fwd.at[to, 0], r_in.at[into, 0, j], device),
            remote(d, d, s_fwd.at[to, 1], r_in.at[into, 1, j], device),
        ]

    def arrived(j, k):
        for copy in onward(j, k, 0, k, (sn, zm)):
            copy.wait_recv()

    def rhs_piece(j):
        at = pl.ds(j * CHUNK, CHUNK)
        return remote(rl.at[at], rin.at[at], s_rhs, r_rhs.at[j], (other, zo))

    def send_own(j):
        @pl.when(hub)
        def _():
            for copy in own(j, 0, 2, (sn, zm)) + own(j, 1, 0, (other, z)):
                copy.start()

        @pl.when(guest)
        def _():
            rhs_piece(j).start()
            for copy in own(j, 0, 1, (sn, zo)):
                copy.start()

    send_own(0)
    to_guest = remote(st, stv, s_st, r_st, (other, z))

    @pl.when(hub)
    def _():
        to_guest.start()

    def share_rhs(k):
        return remote(rt.at[0, at_cols(k)], rtop.at[c], s_rt.at[k], r_rt.at[c], worker(k))

    def rhs_from(m):
        return remote(rtop.at[m], rtop.at[m], s_rt.at[0], r_rt.at[m], (4 * g + m, zo))

    def not_me(k):
        return jnp.logical_or(guest, place != k)

    def not_own(m):
        return jnp.logical_or(guest, c != m)

    for k in range(4):

        @pl.when(not_me(k))
        def _(k=k):
            share_rhs(k).start()

    for j in range(1, min(AHEAD, chunks)):
        send_own(j)

    def top_z(i):
        there = (sn, lax.rem(z + i, 4))
        copies = [remote(td.at[0], tg.at[c, 0, z], s_top.at[i], r_top.at[i], there)]
        for l in range(1, 6):
            copies.append(remote(tb.at[ancestors[l], 0], tg.at[c, l, z], s_top.at[i], r_top.at[i], there))
        return copies

    def top_z_all(i):
        src = lax.rem(z + 4 - i, 4)
        view = tg.at[c, :, src]
        return remote(view, view, s_top.at[i], r_top.at[i], (sn, lax.rem(z + i, 4)))

    for i in range(1, 4):
        for copy in top_z(i):
            copy.start()

    def share_group(i):
        return remote(tg.at[c], tg.at[c], s_grp.at[i], r_grp.at[i], (sibling(i), z))

    def share_upper():
        there = (4 * solver + c, z)
        return [
            remote(tg.at[3, 0], upper.at[g, 0], s_up, r_up.at[g], there),
            remote(tg.at[3, pl.ds(3, 3)], upper.at[g, pl.ds(1, 3)], s_up, r_up.at[g], there),
        ]

    def upper_all(at):
        return remote(upper.at[at], upper.at[at], s_up, r_up.at[at], (4 * solver + c, z))

    for copy in locals_:
        copy.wait()

    @pl.when(hub)
    def _():
        for copy in hub_locals:
            copy.wait()

    @pl.when(guest)
    def _():
        to_guest.wait_recv()

    into_smem = pltpu.make_async_copy(stv, slot_ref, l_sem.at[11])
    into_smem.start()
    into_smem.wait()

    def slot_of(s, r):
        v = slot_ref[s, r]
        t = v - (leaf - 1)
        level = 0
        for l in range(1, 6):
            level = level + jnp.where((t & ((1 << l) - 1)) == 0, 1, 0)
        return jnp.where(v < leaf, v, leaf + level)

    def leaf_block(s):
        return blk[s].reshape(3 * w, w), dinv[s].reshape(w, w)

    def forward_step(s):
        b, d = leaf_block(s)
        solved = dot3(rin[s] + acc[s], d, True)
        fwd[s] = solved
        out = dot3(solved, b, True)
        acc[s + 1] = acc[s + 1] - out[:, :w]
        first, second = slot_of(s, 1), slot_of(s, 2)
        out1, out2 = out[:, w : 2 * w], out[:, 2 * w :]

        def push(t):
            m1 = (first == t).astype(f32)
            m2 = (second == t).astype(f32)
            acc[t] = acc[t] - (m1 * out1 + m2 * out2)

        for t in range(2, leaf + 6):
            push(t)

    def turn(j, carry):
        @pl.when(j + AHEAD < chunks)
        def _():
            send_own(j + AHEAD)

        @pl.when(hub)
        def _():
            @pl.when(j < chunks)
            def _():
                arrived(j, 1)
                for copy in onward(j, 1, 0, 3, (sn, zm)) + onward(j, 1, 1, 1, (other, z)):
                    copy.start()
                arrived(j, 2)
                for copy in onward(j, 2, 2, 2, (other, z)):
                    copy.start()

            @pl.when(j >= LAG)
            def _():
                arrived(j - LAG, 3)
                for copy in onward(j - LAG, 3, 3, 3, (other, z)):
                    copy.start()

        @pl.when(j == min(TOP_Z, chunks))
        def _():
            for i in range(1, 4):
                top_z_all(i).wait_recv()
            for i in range(1, 4):
                share_group(i).start()

        @pl.when(j == min(TOP_GROUP, chunks))
        def _():
            for i in range(1, 4):
                share_group(i).wait_recv()

            @pl.when(jnp.logical_not(is_solver))
            def _():
                for copy in share_upper():
                    copy.start()

        @pl.when(j >= LAG)
        def _():
            @pl.when(guest)
            def _():
                rhs_piece(j - LAG).wait_recv()
                for k in range(4):
                    arrived(j - LAG, k)

            for i in range(CHUNK):
                forward_step((j - LAG) * CHUNK + i)

        return carry

    lax.fori_loop(0, chunks + LAG, turn, 0)

    def share_part(i):
        to, device = mate(place, i)
        return remote(acc.at[pl.ds(leaf, 6), at_cols(to)], part.at[place], s_part.at[i], r_part.at[i], device)

    for i in range(1, 4):
        share_part(i).start()
    part[place] = acc[pl.ds(leaf, 6), my_cols]

    for m in range(4):

        @pl.when(not_own(m))
        def _(m=m):
            rhs_from(m).wait_recv()

    for i in range(1, 4):
        share_part(i).wait_recv()

    def top_block(m, l):
        return tg[m, l].reshape(w, w)

    def top_stack(m):
        return tg[m, 2:6].reshape(4 * w, w)

    path = part[0] + part[1] + part[2] + part[3]
    f0 = dot3(path[0] + rtop[0], top_block(0, 0), True)
    f1 = dot3(path[1] + rtop[1] - dot3(f0, top_block(0, 1), True), top_block(1, 0), True)
    f2 = dot3(rtop[2], top_block(2, 0), True)
    out = dot3(f0, top_stack(0), True) + dot3(f1, top_stack(1), True) + dot3(f2, top_stack(2), True)
    ftop[0], ftop[1], ftop[2] = f0, f1, f2
    last = 4 * g + 3
    above = [(last + 1) % (1 << l) == 0 for l in range(6)]
    for l in range(2, 6):
        mine = above[l]
        if l < 5:
            mine = jnp.logical_and(mine, jnp.logical_not(above[l + 1]))
        contrib[l - 2] = path[l] + mine.astype(f32) * rtop[3] - out[:, (l - 2) * w : (l - 1) * w]

    def share_contrib():
        return remote(contrib, gathered.at[g], s_con, r_con.at[g], (4 * solver + c, z))

    def contrib_from(at):
        return remote(gathered.at[at], gathered.at[at], s_con, r_con.at[at], (4 * solver + c, z))

    def share_x(i):
        to = lax.rem(g + i, 8)
        return remote(xs.at[to], xpath, s_x.at[i], r_x, (classmate(i), z))

    @pl.when(jnp.logical_not(is_solver))
    def _():
        share_contrib().start()

    @pl.when(is_solver)
    def _():
        upper[g, 0] = tg[3, 0]
        upper[g, 1:4] = tg[3, 3:6]
        gathered[g] = contrib[...]
        for i in range(1, 8):
            at = lax.rem(g + i, 8)
            upper_all(at).wait_recv()
            contrib_from(at).wait_recv()

        def upper_block(q, slot):
            return upper[q, slot].reshape(w, w)

        spans = [range(q + 1 - (1 << trailing(q)), q) for q in range(8)]
        order = sorted(range(8), key=lambda q: (trailing(q), q))
        forward = {}
        for q in order:
            level = trailing(q)
            source = gathered[q, level]
            for below in spans[q]:
                source = source + gathered[below, level]
            for below in spans[q]:
                source = source - dot3(forward[below], upper_block(below, level), True)
            forward[q] = dot3(source, upper_block(q, 0), True)
        solved = {}
        for q in reversed(order):
            source = forward[q]
            for up in range(q + 1, 8):
                if q in spans[up]:
                    source = source - dot3(solved[up], upper_block(q, trailing(up)), False)
            solved[q] = dot3(source, upper_block(q, 0), False)
        for to in range(8):
            for level in range(4):
                q = (to >> level) * (1 << level) + (1 << level) - 1
                if trailing(q) == level:
                    xs[to, level] = solved[q]
                else:
                    xs[to, level] = jnp.zeros((cc, w), f32)
        for i in range(1, 8):
            share_x(i).start()
        xpath[...] = xs[g]

    @pl.when(jnp.logical_not(is_solver))
    def _():
        remote(xpath, xpath, s_x.at[0], r_x, (4 * solver + c, z)).wait_recv()

    across = jnp.concatenate([xpath[0], xpath[1], xpath[2], xpath[3]], axis=1)
    x1 = dot3(ftop[1] - dot3(across, top_stack(1), False), top_block(1, 0), False)
    x2 = dot3(ftop[2] - dot3(across, top_stack(2), False), top_block(2, 0), False)
    x0 = dot3(
        ftop[0] - dot3(across, top_stack(0), False) - dot3(x1, top_block(0, 1), False), top_block(0, 0), False
    )
    zown[0], zown[1], zown[6] = x0, x1, x2
    zown[2:6] = xpath[...]

    def share_z(i):
        to, device = mate(place, i)
        return remote(zown.at[pl.ds(0, 6)], zbuf.at[pl.ds(leaf, 6), my_cols], s_z.at[i], r_z.at[i], device)

    def z_from(i):
        view = zbuf.at[pl.ds(leaf, 6), at_cols(lax.rem(place + 4 - i, 4))]
        return remote(zown.at[pl.ds(0, 6)], view, s_z.at[i], r_z.at[i], mate(place, i)[1])

    for i in range(1, 4):
        share_z(i).start()
    zbuf[pl.ds(leaf, 6), my_cols] = zown[0:6]

    def level_of(t):
        return sum(jnp.where((t + 1) % (1 << l) == 0, 1, 0) for l in range(1, 6))

    top_slots = (0, 1, 6, level_of(last))

    def share_top(m):
        return remote(zown.at[top_slots[m]], tout.at[my_cols], s_to.at[m], r_to.at[place], (4 * g + m, block))

    def top_from(k):
        return remote(zown.at[0], tout.at[at_cols(k)], s_to.at[0], r_to.at[k], worker(k))

    for m in range(4):

        @pl.when(not_own(m))
        def _(m=m):
            share_top(m).start()

    @pl.when(hub)
    def _():
        tout[my_cols] = zown[jnp.where(c == 2, 6, level_of(sn))]

    for i in range(1, 4):
        z_from(i).wait_recv()

    def back_piece(j):
        at = pl.ds(leaf - (j + 1) * CHUNK, CHUNK)
        return remote(zbuf.at[at], o_leaf.at[at], s_back, r_back, (other, zo))

    def keep_piece(j):
        at = pl.ds(leaf - (j + 1) * CHUNK, CHUNK)
        return pltpu.make_async_copy(zbuf.at[at], o_leaf.at[at], l_sem.at[0])

    def let_go(j):
        @pl.when(hub)
        def _():
            keep_piece(j).start()

        @pl.when(guest)
        def _():
            back_piece(j).start()

    def backward(j, carry):
        for i in range(CHUNK):
            s = leaf - 1 - j * CHUNK - i
            b, d = leaf_block(s)
            z_at = jnp.concatenate([zbuf[s + 1], zbuf[slot_of(s, 1)], zbuf[slot_of(s, 2)]], axis=1)
            zbuf[s] = dot3(fwd[s] - dot3(z_at, b, False), d, False)

        @pl.when(j >= 1)
        def _():
            let_go(j - 1)

        return carry

    lax.fori_loop(0, chunks, backward, 0)

    for k in range(4):

        @pl.when(not_me(k))
        def _(k=k):
            top_from(k).wait_recv()

    top_out = pltpu.make_async_copy(tout, o_top.at[0], l_sem.at[1])
    top_out.start()
    let_go(chunks - 1)

    whole = pl.ds(0, leaf)

    def left(ssem, rows):
        b, d = blk.at[:, :, rows], dinv.at[:, rows]
        remote(b, b, ssem.at[0], r_in.at[0, 0, 0], (sn, zo)).wait_send()
        remote(d, d, ssem.at[1], r_in.at[0, 1, 0], (sn, zo)).wait_send()

    left(s_own.at[0], z)
    for i in range(1, 4):
        top_z_all(i).wait_send()
        share_group(i).wait_send()
        share_part(i).wait_send()
        share_z(i).wait_send()
    for m in range(4):

        @pl.when(not_me(m))
        def _(m=m):
            share_rhs(m).wait_send()

        @pl.when(not_own(m))
        def _(m=m):
            share_top(m).wait_send()

    @pl.when(jnp.logical_not(is_solver))
    def _():
        upper_all(g).wait_send()
        share_contrib().wait_send()

    @pl.when(is_solver)
    def _():
        for i in range(1, 8):
            share_x(i).wait_send()

    @pl.when(hub)
    def _():
        left(s_own.at[1], z)
        for to in range(4):
            left(s_fwd.at[to], z)
        to_guest.wait_send()
        pltpu.make_async_copy(zbuf.at[whole], o_leaf, l_sem.at[0]).wait()

    @pl.when(guest)
    def _():
        remote(rl, rin, s_rhs, r_rhs.at[0], (other, zo)).wait_send()
        everything = remote(zbuf.at[whole], o_leaf, s_back, r_back, (other, zo))
        everything.wait_send()
        everything.wait_recv()

    top_out.wait()


def local(rl, rt, lb, ld, st, tb, td):
    leaf, cols, w = rl.shape
    cc, quarter, chunks = cols // 4, w // 4, leaf // CHUNK
    any_spec = pl.BlockSpec(memory_space=pl.ANY)
    dma = pltpu.SemaphoreType.DMA
    return pl.pallas_call(
        kernel,
        out_shape=(jax.ShapeDtypeStruct(rl.shape, f32), jax.ShapeDtypeStruct(rt.shape, f32)),
        in_specs=[any_spec] * 7,
        out_specs=(any_spec, any_spec),
        scratch_shapes=[
            pltpu.VMEM((leaf + 6, cols, w), f32),
            pltpu.VMEM((leaf, cols, w), f32),
            pltpu.VMEM((leaf, 3, 4, quarter, w), f32),
            pltpu.VMEM((leaf, 4, quarter, w), f32),
            pltpu.VMEM((leaf, cols, w), f32),
            pltpu.VMEM((leaf + 6, cols, w), f32),
            pltpu.VMEM((4, 6, 4, quarter, w), f32),
            pltpu.VMEM((4, cc, w), f32),
            pltpu.VMEM((4, 6, cc, w), f32),
            pltpu.VMEM((4, cc, w), f32),
            pltpu.VMEM((8, 4, cc, w), f32),
            pltpu.VMEM((8, 4, 4, quarter, w), f32),
            pltpu.VMEM((8, 4, cc, w), f32),
            pltpu.VMEM((4, cc, w), f32),
            pltpu.VMEM((7, cc, w), f32),
            pltpu.VMEM((3, cc, w), f32),
            pltpu.VMEM((cols, w), f32),
            pltpu.VMEM(st.shape, jnp.int32),
            pltpu.SMEM(st.shape, jnp.int32),
            dma((2, 2)), dma((4, 2)), dma, dma, dma((4, 2, chunks)), dma((chunks,)), dma,
            dma((4,)), dma((4,)), dma((4,)), dma((4,)), dma((4,)), dma((4,)),
            dma, dma((8,)), dma((4,)), dma((4,)), dma, dma((8,)), dma((8,)), dma, dma((4,)), dma((4,)),
            dma((4,)), dma((4,)), dma, dma, dma((12,)),
        ],
        compiler_params=pltpu.CompilerParams(
            collective_id=0, has_side_effects=True, vmem_limit_bytes=60 * 1024 * 1024
        ),
        name="substitution",
    )(st, rl, rt, lb, ld, tb, td)


def solution(mesh):
    return jax.shard_map(
        local,
        mesh=mesh,
        in_specs=(
            P("sn", "rhs", None),
            P("sn", "rhs", None),
            P("sn", None, "rhs", None),
            P("sn", "rhs", None),
            P("sn", None),
            P(None, "sn", "rhs", None),
            P("sn", "rhs", None),
        ),
        out_specs=(P("sn", "rhs", None), P("sn", "rhs", None)),
        check_vma=False,
    )
```

```python
import functools

import jax
import jax.numpy as jnp
from jax import lax
from jax.experimental import pallas as pl
from jax.experimental.pallas import tpu as pltpu
from jax.sharding import PartitionSpec as P

MESH = pl.DeviceIdType.MESH
f32 = jnp.float32
bf16 = jnp.bfloat16

CHUNK = 2
AHEAD = 3
LAG = 2
TOP_TURNS = 1, 3, 7, 8


def split(x):
    high = x.astype(bf16)
    return high, (x - high.astype(f32)).astype(bf16)


def dot3(x, w, transposed):
    dims = (((1,), (1 if transposed else 0,)), ((), ()))
    dot = functools.partial(lax.dot_general, dimension_numbers=dims, preferred_element_type=f32)
    x_high, x_low = split(x)
    w_high, w_low = split(w)
    return dot(x_high, w_high) + (dot(x_high, w_low) + dot(x_low, w_high))


def trailing(q):
    count = 0
    while (q >> count) & 1:
        count += 1
    return count


def kernel(
    st, rl, rt, lb, ld, tb, td,
    o_leaf, o_top,
    acc, rin, blk, dinv, fwd, zbuf, tg, rtop, part, contrib, gathered, upper, xs, xpath, zown, ftop, tout, stv, slot_ref,
    s_own, s_fwd, s_rhs, s_back, r_in, r_rhs, r_back,
    s_top, r_top, s_rt, r_rt, s_grp, r_grp, s_up, r_up, s_part, r_part, s_con, r_con, s_z, r_z, s_to, r_to,
    s_st, r_st, l_sem,
):
    leaf, cols, w = rl.shape
    quarter = w // 4
    cc = cols // 4
    chunks = leaf // CHUNK
    sn, z = lax.axis_index("sn"), lax.axis_index("rhs")
    g, c = sn // 4, sn % 4
    core, low = sn % 2, z // 2
    hub = core == low
    guest = jnp.logical_not(hub)
    role = jnp.where(hub, 0, 1)
    other, zm, zo = sn + 1 - 2 * core, z + 1 - 2 * (z % 2), 3 - z
    rows_of = (z, zo, zm, 3 - zm)
    place = 2 * (c // 2) + role
    block = jnp.where(hub, z, zo)

    def at_cols(k):
        return pl.ds(pl.multiple_of(k * cc, cc), cc)

    my_cols = at_cols(place)

    def sibling(i):
        return 4 * g + lax.rem(c + i, 4)

    def classmate(i):
        return 4 * lax.rem(g + i, 8) + c

    def mate(k, i):
        to = lax.rem(k + i, 4)
        return to, (4 * g + 2 * (to // 2) + core, jnp.where(to % 2 == role, z, zo))

    def worker(k):
        return 4 * g + 2 * (k // 2) + low, (z if k % 2 == 0 else zo)

    def remote(src, dst, ssem, rsem, device):
        return pltpu.make_async_remote_copy(
            src_ref=src, dst_ref=dst, send_sem=ssem, recv_sem=rsem, device_id=device, device_id_type=MESH
        )

    barrier = pltpu.get_barrier_semaphore()

    def greet(device):
        pl.semaphore_signal(barrier, inc=1, device_id=device, device_id_type=MESH)

    for i in range(1, 4):
        greet((sibling(i), z))
    for i in range(4):
        greet((sibling(i), zo))
    greet((sn, zm))
    greet((sn, 3 - zm))
    for i in range(1, 8):
        greet((classmate(i), z))

    locals_ = [pltpu.make_async_copy(td.at[0], tg.at[c, 0, z], l_sem.at[0])]
    ancestors = [(sn >> l) * (1 << l) + ((1 << l) - 1) for l in range(6)]
    for l in range(1, 6):
        locals_.append(pltpu.make_async_copy(tb.at[ancestors[l], 0], tg.at[c, l, z], l_sem.at[l]))
    hub_locals = [
        pltpu.make_async_copy(rl, rin, l_sem.at[6]),
        pltpu.make_async_copy(lb, blk.at[:, :, z], l_sem.at[7]),
        pltpu.make_async_copy(ld, dinv.at[:, z], l_sem.at[8]),
        pltpu.make_async_copy(st, stv, l_sem.at[9]),
        pltpu.make_async_copy(rt.at[0, my_cols], rtop.at[c], l_sem.at[10]),
    ]
    for copy in locals_:
        copy.start()

    @pl.when(hub)
    def _():
        for copy in hub_locals:
            copy.start()

    def clear(t, carry):
        acc[t] = jnp.zeros((cols, w), f32)
        return carry

    lax.fori_loop(0, leaf + 6, clear, 0)
    pl.semaphore_wait(barrier, 16)

    def piece(j, k):
        at = pl.ds(j * CHUNK, CHUNK)
        return blk.at[at, :, rows_of[k]], dinv.at[at, rows_of[k]]

    def own(j, to, k, device):
        at = pl.ds(j * CHUNK, CHUNK)
        return [
            remote(lb.at[at], blk.at[at, :, z], s_own.at[to, 0], r_in.at[k, 0, j], device),
            remote(ld.at[at], dinv.at[at, z], s_own.at[to, 1], r_in.at[k, 1, j], device),
        ]

    def onward(j, k, to, into, device):
        b, d = piece(j, k)
        return [
            remote(b, b, s_fwd.at[to, 0], r_in.at[into, 0, j], device),
            remote(d, d, s_fwd.at[to, 1], r_in.at[into, 1, j], device),
        ]

    def arrived(j, k):
        for copy in onward(j, k, 0, k, (sn, zm)):
            copy.wait_recv()

    def rhs_piece(j):
        at = pl.ds(j * CHUNK, CHUNK)
        return remote(rl.at[at], rin.at[at], s_rhs, r_rhs.at[j], (other, zo))

    def send_own(j):
        @pl.when(hub)
        def _():
            for copy in own(j, 0, 2, (sn, zm)) + own(j, 1, 0, (other, z)):
                copy.start()

        @pl.when(guest)
        def _():
            rhs_piece(j).start()
            for copy in own(j, 0, 1, (sn, zo)):
                copy.start()

    send_own(0)

    def top_z(i):
        there = (sn, (zm, zo)[i])
        copies = [remote(td.at[0], tg.at[c, 0, z], s_top.at[i], r_top.at[i], there)]
        for l in range(1, 6):
            copies.append(remote(tb.at[ancestors[l], 0], tg.at[c, l, z], s_top.at[i], r_top.at[i], there))
        return copies

    def top_z_all(i):
        view = tg.at[c, :, (zm, zo, zm)[i]]
        return remote(view, view, s_top.at[i], r_top.at[i], (sn, (zm, zo, zo)[i]))

    for i in range(2):
        for copy in top_z(i):
            copy.start()

    to_guest = remote(st, stv, s_st, r_st, (other, z))

    @pl.when(hub)
    def _():
        to_guest.start()

    def share_rhs(k):
        return remote(rt.at[0, at_cols(k)], rtop.at[c], s_rt.at[k], r_rt.at[c], worker(k))

    def rhs_from(m):
        return remote(rtop.at[m], rtop.at[m], s_rt.at[0], r_rt.at[m], (4 * g + m, zo))

    def not_me(k):
        return jnp.logical_or(guest, place != k)

    def not_own(m):
        return jnp.logical_or(guest, c != m)

    for k in range(4):

        @pl.when(not_me(k))
        def _(k=k):
            share_rhs(k).start()

    for j in range(1, min(AHEAD, chunks)):
        send_own(j)

    def share_group(i):
        what = (c, c, lax.rem(c + 2, 4))[i]
        there = (4 * g + lax.rem(c + 2, 4), other, other)[i]
        return remote(tg.at[what], tg.at[what], s_grp.at[i], r_grp.at[i], (there, z))

    def exists(q, level):
        return (q // (1 << level)) % 2 == 0

    def share_upper(i, slot):
        return remote(
            tg.at[3, slot if slot == 0 else slot + 2], upper.at[g, slot], s_up.at[i, slot], r_up.at[g, slot],
            (classmate(i), z),
        )

    def upper_from(at, slot):
        view = upper.at[at, slot]
        return remote(view, view, s_up.at[0, slot], r_up.at[at, slot], (4 * at + c, z))

    def has_upper(q, slot):
        return jnp.logical_and(exists(q, slot), (q + 1) % (1 << slot) != 0)

    for copy in locals_:
        copy.wait()

    @pl.when(hub)
    def _():
        for copy in hub_locals:
            copy.wait()

    @pl.when(guest)
    def _():
        to_guest.wait_recv()

    into_smem = pltpu.make_async_copy(stv, slot_ref, l_sem.at[11])
    into_smem.start()
    into_smem.wait()

    def slot_of(s, r):
        v = slot_ref[r, s]
        t = v - (leaf - 1)
        level = 0
        for l in range(1, 6):
            level = level + jnp.where((t & ((1 << l) - 1)) == 0, 1, 0)
        return jnp.where(v < leaf, v, leaf + level)

    def leaf_block(s):
        return blk[s].reshape(3 * w, w), dinv[s].reshape(w, w)

    def forward_step(s):
        b, d = leaf_block(s)
        solved = dot3(rin[s] + acc[s], d, True)
        fwd[s] = solved
        out = dot3(solved, b, True)
        acc[s + 1] = acc[s + 1] - out[:, :w]
        first, second = slot_of(s, 1), slot_of(s, 2)
        out1, out2 = out[:, w : 2 * w], out[:, 2 * w :]

        def push(t):
            m1 = (first == t).astype(f32)
            m2 = (second == t).astype(f32)
            acc[t] = acc[t] - (m1 * out1 + m2 * out2)

        for t in range(2, leaf + 6):
            push(t)

    def turn(j, carry):
        @pl.when(j + AHEAD < chunks)
        def _():
            send_own(j + AHEAD)

        @pl.when(hub)
        def _():
            @pl.when(j < chunks)
            def _():
                arrived(j, 1)
                for copy in onward(j, 1, 0, 3, (sn, zm)) + onward(j, 1, 1, 1, (other, z)):
                    copy.start()
                arrived(j, 2)
                for copy in onward(j, 2, 2, 2, (other, z)):
                    copy.start()

            @pl.when(j >= LAG)
            def _():
                arrived(j - LAG, 3)
                for copy in onward(j - LAG, 3, 3, 3, (other, z)):
                    copy.start()

        @pl.when(j == TOP_TURNS[0])
        def _():
            top_z_all(0).wait_recv()
            top_z_all(2).start()

        @pl.when(j == TOP_TURNS[1])
        def _():
            top_z_all(1).wait_recv()
            top_z_all(2).wait_recv()
            for i in range(2):
                share_group(i).start()

        @pl.when(j == TOP_TURNS[2])
        def _():
            share_group(0).wait_recv()
            share_group(2).start()

        @pl.when(j == TOP_TURNS[3])
        def _():
            share_group(1).wait_recv()
            share_group(2).wait_recv()
            for i in range(1, 8):
                share_upper(i, 0).start()
            for slot in range(1, 4):

                @pl.when(has_upper(g, slot))
                def _(slot=slot):
                    for i in range(1, 8):
                        share_upper(i, slot).start()

        @pl.when(j >= LAG)
        def _():
            @pl.when(guest)
            def _():
                rhs_piece(j - LAG).wait_recv()
                for k in range(4):
                    arrived(j - LAG, k)

            for i in range(CHUNK):
                forward_step((j - LAG) * CHUNK + i)

        return carry

    lax.fori_loop(0, chunks + LAG, turn, 0)

    def share_part(i):
        to, device = mate(place, i)
        return remote(acc.at[pl.ds(leaf, 6), at_cols(to)], part.at[place], s_part.at[i], r_part.at[i], device)

    for i in range(1, 4):
        share_part(i).start()
    part[place] = acc[pl.ds(leaf, 6), my_cols]

    for m in range(4):

        @pl.when(not_own(m))
        def _(m=m):
            rhs_from(m).wait_recv()

    for i in range(1, 4):
        share_part(i).wait_recv()

    def top_block(m, l):
        return tg[m, l].reshape(w, w)

    def top_stack(m):
        return tg[m, 2:6].reshape(4 * w, w)

    path = part[0] + part[1] + part[2] + part[3]
    f0 = dot3(path[0] + rtop[0], top_block(0, 0), True)
    f1 = dot3(path[1] + rtop[1] - dot3(f0, top_block(0, 1), True), top_block(1, 0), True)
    f2 = dot3(rtop[2], top_block(2, 0), True)
    out = dot3(f0, top_stack(0), True) + dot3(f1, top_stack(1), True) + dot3(f2, top_stack(2), True)
    ftop[0], ftop[1], ftop[2] = f0, f1, f2
    last = 4 * g + 3
    above = [(last + 1) % (1 << l) == 0 for l in range(6)]
    for l in range(2, 6):
        mine = above[l]
        if l < 5:
            mine = jnp.logical_and(mine, jnp.logical_not(above[l + 1]))
        contrib[l - 2] = path[l] + mine.astype(f32) * rtop[3] - out[:, (l - 2) * w : (l - 1) * w]

    def share_contrib(i, level):
        return remote(
            contrib.at[level], gathered.at[g, level], s_con.at[i, level], r_con.at[g, level], (classmate(i), z)
        )

    def contrib_from(at, level):
        view = gathered.at[at, level]
        return remote(view, view, s_con.at[0, level], r_con.at[at, level], (4 * at + c, z))

    for level in range(4):

        @pl.when(exists(g, level))
        def _(level=level):
            for i in (4, 3, 5, 2, 6, 1, 7):
                share_contrib(i, level).start()

    upper[g, 0] = tg[3, 0]
    upper[g, 1:4] = tg[3, 3:6]
    gathered[g] = contrib[...]
    for i in range(1, 8):
        at = lax.rem(g + i, 8)
        upper_from(at, 0).wait_recv()
        for slot in range(1, 4):

            @pl.when(has_upper(at, slot))
            def _(at=at, slot=slot):
                upper_from(at, slot).wait_recv()

    for i in range(1, 8):
        at = lax.rem(g + i, 8)
        for level in range(4):

            @pl.when(exists(at, level))
            def _(at=at, level=level):
                contrib_from(at, level).wait_recv()

    def upper_block(q, slot):
        return upper[q, slot].reshape(w, w)

    spans = [range(q + 1 - (1 << trailing(q)), q) for q in range(8)]
    order = sorted(range(8), key=lambda q: (trailing(q), q))
    forward = {}
    for q in order:
        level = trailing(q)
        source = gathered[q, level]
        for below in spans[q]:
            source = source + gathered[below, level]
        for below in spans[q]:
            source = source - dot3(forward[below], upper_block(below, level), True)
        forward[q] = dot3(source, upper_block(q, 0), True)
    solved = {}
    for q in reversed(order):
        source = forward[q]
        for up in range(q + 1, 8):
            if q in spans[up]:
                source = source - dot3(solved[up], upper_block(q, trailing(up)), False)
        solved[q] = dot3(source, upper_block(q, 0), False)
        xs[q] = solved[q]
    for level in range(4):
        q = (g // (1 << level)) * (1 << level) + (1 << level) - 1
        xpath[level] = xs[q] * exists(g, level).astype(f32)

    across = jnp.concatenate([xpath[0], xpath[1], xpath[2], xpath[3]], axis=1)
    x1 = dot3(ftop[1] - dot3(across, top_stack(1), False), top_block(1, 0), False)
    x2 = dot3(ftop[2] - dot3(across, top_stack(2), False), top_block(2, 0), False)
    x0 = dot3(
        ftop[0] - dot3(across, top_stack(0), False) - dot3(x1, top_block(0, 1), False), top_block(0, 0), False
    )
    zown[0], zown[1], zown[6] = x0, x1, x2
    zown[2:6] = xpath[...]

    def share_z(i):
        to, device = mate(place, i)
        return remote(zown.at[pl.ds(0, 6)], zbuf.at[pl.ds(leaf, 6), my_cols], s_z.at[i], r_z.at[i], device)

    def z_from(i):
        view = zbuf.at[pl.ds(leaf, 6), at_cols(lax.rem(place + 4 - i, 4))]
        return remote(zown.at[pl.ds(0, 6)], view, s_z.at[i], r_z.at[i], mate(place, i)[1])

    for i in range(1, 4):
        share_z(i).start()
    zbuf[pl.ds(leaf, 6), my_cols] = zown[0:6]

    def level_of(t):
        return sum(jnp.where((t + 1) % (1 << l) == 0, 1, 0) for l in range(1, 6))

    top_slots = (0, 1, 6, level_of(last))

    def share_top(m):
        return remote(zown.at[top_slots[m]], tout.at[my_cols], s_to.at[m], r_to.at[place], (4 * g + m, block))

    def top_from(k):
        return remote(zown.at[0], tout.at[at_cols(k)], s_to.at[0], r_to.at[k], worker(k))

    for m in range(4):

        @pl.when(not_own(m))
        def _(m=m):
            share_top(m).start()

    @pl.when(hub)
    def _():
        tout[my_cols] = zown[jnp.where(c == 2, 6, level_of(sn))]

    for i in range(1, 4):
        z_from(i).wait_recv()

    def back_piece(j):
        at = pl.ds(leaf - (j + 1) * CHUNK, CHUNK)
        return remote(zbuf.at[at], o_leaf.at[at], s_back, r_back, (other, zo))

    def keep_piece(j):
        at = pl.ds(leaf - (j + 1) * CHUNK, CHUNK)
        return pltpu.make_async_copy(zbuf.at[at], o_leaf.at[at], l_sem.at[0])

    def let_go(j):
        @pl.when(hub)
        def _():
            keep_piece(j).start()

        @pl.when(guest)
        def _():
            back_piece(j).start()

    def backward(j, carry):
        for i in range(CHUNK):
            s = leaf - 1 - j * CHUNK - i
            b, d = leaf_block(s)
            z_at = jnp.concatenate([zbuf[s + 1], zbuf[slot_of(s, 1)], zbuf[slot_of(s, 2)]], axis=1)
            zbuf[s] = dot3(fwd[s] - dot3(z_at, b, False), d, False)

        @pl.when(j >= 1)
        def _():
            let_go(j - 1)

        return carry

    lax.fori_loop(0, chunks, backward, 0)

    for k in range(4):

        @pl.when(not_me(k))
        def _(k=k):
            top_from(k).wait_recv()

    top_out = pltpu.make_async_copy(tout, o_top.at[0], l_sem.at[1])
    top_out.start()
    let_go(chunks - 1)

    whole = pl.ds(0, leaf)

    def left(ssem, rows):
        b, d = blk.at[:, :, rows], dinv.at[:, rows]
        remote(b, b, ssem.at[0], r_in.at[0, 0, 0], (sn, zo)).wait_send()
        remote(d, d, ssem.at[1], r_in.at[0, 1, 0], (sn, zo)).wait_send()

    left(s_own.at[0], z)
    for i in range(3):
        top_z_all(i).wait_send()
        share_group(i).wait_send()
        share_part(i + 1).wait_send()
        share_z(i + 1).wait_send()
    for m in range(4):

        @pl.when(not_me(m))
        def _(m=m):
            share_rhs(m).wait_send()

        @pl.when(not_own(m))
        def _(m=m):
            share_top(m).wait_send()

    for i in range(1, 8):
        share_upper(i, 0).wait_send()
    for slot in range(1, 4):

        @pl.when(has_upper(g, slot))
        def _(slot=slot):
            for i in range(1, 8):
                share_upper(i, slot).wait_send()

    for level in range(4):

        @pl.when(exists(g, level))
        def _(level=level):
            for i in range(1, 8):
                share_contrib(i, level).wait_send()

    @pl.when(hub)
    def _():
        left(s_own.at[1], z)
        for to in range(4):
            left(s_fwd.at[to], z)
        to_guest.wait_send()
        pltpu.make_async_copy(zbuf.at[whole], o_leaf, l_sem.at[0]).wait()

    @pl.when(guest)
    def _():
        remote(rl, rin, s_rhs, r_rhs.at[0], (other, zo)).wait_send()
        everything = remote(zbuf.at[whole], o_leaf, s_back, r_back, (other, zo))
        everything.wait_send()
        everything.wait_recv()

    top_out.wait()


def local(rl, rt, lb, ld, st, tb, td):
    leaf, cols, w = rl.shape
    cc, quarter, chunks = cols // 4, w // 4, leaf // CHUNK
    any_spec = pl.BlockSpec(memory_space=pl.ANY)
    operands = [pltpu.with_memory_space_constraint(v, pltpu.HBM) for v in (st.T, rl, rt, lb, ld, tb, td)]
    dma = pltpu.SemaphoreType.DMA
    return pl.pallas_call(
        kernel,
        out_shape=(jax.ShapeDtypeStruct(rl.shape, f32), jax.ShapeDtypeStruct(rt.shape, f32)),
        in_specs=[any_spec] * 7,
        out_specs=(pl.BlockSpec(memory_space=pltpu.VMEM),) * 2,
        scratch_shapes=[
            pltpu.VMEM((leaf + 6, cols, w), f32),
            pltpu.VMEM((leaf, cols, w), f32),
            pltpu.VMEM((leaf, 3, 4, quarter, w), f32),
            pltpu.VMEM((leaf, 4, quarter, w), f32),
            pltpu.VMEM((leaf, cols, w), f32),
            pltpu.VMEM((leaf + 6, cols, w), f32),
            pltpu.VMEM((4, 6, 4, quarter, w), f32),
            pltpu.VMEM((4, cc, w), f32),
            pltpu.VMEM((4, 6, cc, w), f32),
            pltpu.VMEM((4, cc, w), f32),
            pltpu.VMEM((8, 4, cc, w), f32),
            pltpu.VMEM((8, 4, 4, quarter, w), f32),
            pltpu.VMEM((8, cc, w), f32),
            pltpu.VMEM((4, cc, w), f32),
            pltpu.VMEM((7, cc, w), f32),
            pltpu.VMEM((3, cc, w), f32),
            pltpu.VMEM((cols, w), f32),
            pltpu.VMEM(st.shape[::-1], jnp.int32),
            pltpu.SMEM(st.shape[::-1], jnp.int32),
            dma((2, 2)), dma((4, 2)), dma, dma, dma((4, 2, chunks)), dma((chunks,)), dma,
            dma((4,)), dma((4,)), dma((4,)), dma((4,)), dma((4,)), dma((4,)),
            dma((8, 4)), dma((8, 4)), dma((4,)), dma((4,)), dma((8, 4)), dma((8, 4)), dma((4,)), dma((4,)),
            dma((4,)), dma((4,)), dma, dma, dma((12,)),
        ],
        compiler_params=pltpu.CompilerParams(
            collective_id=0, has_side_effects=True, vmem_limit_bytes=24*1024*1024
        ),
        name="substitution",
    )(*operands)


def solution(mesh):
    return jax.shard_map(
        local,
        mesh=mesh,
        in_specs=(
            P("sn", "rhs", None),
            P("sn", "rhs", None),
            P("sn", None, "rhs", None),
            P("sn", "rhs", None),
            P("sn", None),
            P(None, "sn", "rhs", None),
            P("sn", "rhs", None),
        ),
        out_specs=(P("sn", "rhs", None), P("sn", "rhs", None)),
        check_vma=False,
    )
```

```python
import functools

import jax
import jax.numpy as jnp
from jax import lax
from jax.experimental import pallas as pl
from jax.experimental.pallas import tpu as pltpu
from jax.sharding import PartitionSpec as P

MESH = pl.DeviceIdType.MESH
f32 = jnp.float32
bf16 = jnp.bfloat16

CHUNK = 2
AHEAD = 3
LAG = 3
TOP_TURNS = 2, 4, 5, 9, 10


def split(x):
    high = x.astype(bf16)
    return high, (x - high.astype(f32)).astype(bf16)


def dot3(x, w, transposed):
    dims = (((1,), (1 if transposed else 0,)), ((), ()))
    dot = functools.partial(lax.dot_general, dimension_numbers=dims, preferred_element_type=f32)
    x_high, x_low = split(x)
    w_high, w_low = split(w)
    m = x.shape[0]
    both = dot(jnp.concatenate([x_high, x_low], axis=0), w_high)
    return both[:m] + (both[m:] + dot(x_high, w_low))


def trailing(q):
    count = 0
    while (q >> count) & 1:
        count += 1
    return count


def kernel(
    st, rl, rt, lb, ld, tb, td,
    o_leaf, o_top,
    acc, rin, blk, dinv, fwd, zbuf, tg, rtop, part, contrib, gathered, upper, xs, xpath, zown, ftop, tout, stv, slot_ref,
    s_own, s_fwd, s_rhs, s_back, r_in, r_rhs, r_back,
    s_top, r_top, s_rt, r_rt, s_grp, r_grp, s_up, r_up, s_part, r_part, s_con, r_con, s_z, r_z, s_to, r_to,
    s_st, r_st, l_sem,
):
    leaf, cols, w = rl.shape
    quarter = w // 4
    cc = cols // 4
    chunks = leaf // CHUNK
    sn, z = lax.axis_index("sn"), lax.axis_index("rhs")
    g, c = sn // 4, sn % 4
    core, low = sn % 2, z // 2
    hub = core == low
    guest = jnp.logical_not(hub)
    role = jnp.where(hub, 0, 1)
    other, zm, zo = sn + 1 - 2 * core, z + 1 - 2 * (z % 2), 3 - z
    rows_of = (z, zo, zm, 3 - zm)
    place = 2 * (c // 2) + role
    block = jnp.where(hub, z, zo)

    def at_cols(k):
        return pl.ds(pl.multiple_of(k * cc, cc), cc)

    my_cols = at_cols(place)

    def sibling(i):
        return 4 * g + lax.rem(c + i, 4)

    def classmate(i):
        return 4 * lax.rem(g + i, 8) + c

    def mate(k, i):
        to = lax.rem(k + i, 4)
        return to, (4 * g + 2 * (to // 2) + core, jnp.where(to % 2 == role, z, zo))

    def worker(k):
        return 4 * g + 2 * (k // 2) + low, (z if k % 2 == 0 else zo)

    def remote(src, dst, ssem, rsem, device):
        return pltpu.make_async_remote_copy(
            src_ref=src, dst_ref=dst, send_sem=ssem, recv_sem=rsem, device_id=device, device_id_type=MESH
        )

    barrier = pltpu.get_barrier_semaphore()

    def greet(device):
        pl.semaphore_signal(barrier, inc=1, device_id=device, device_id_type=MESH)

    for i in range(1, 4):
        greet((sibling(i), z))
    for i in range(4):
        greet((sibling(i), zo))
    greet((sn, zm))
    greet((sn, 3 - zm))
    for i in range(1, 8):
        greet((classmate(i), z))

    locals_ = [pltpu.make_async_copy(td.at[0], tg.at[c, 0, z], l_sem.at[0])]
    ancestors = [(sn >> l) * (1 << l) + ((1 << l) - 1) for l in range(6)]
    for l in range(1, 6):
        locals_.append(pltpu.make_async_copy(tb.at[ancestors[l], 0], tg.at[c, l, z], l_sem.at[l]))
    hub_locals = [
        pltpu.make_async_copy(rl, rin, l_sem.at[6]),
        pltpu.make_async_copy(lb, blk.at[:, :, z], l_sem.at[7]),
        pltpu.make_async_copy(ld, dinv.at[:, z], l_sem.at[8]),
        pltpu.make_async_copy(st, stv, l_sem.at[9]),
        pltpu.make_async_copy(rt.at[0, my_cols], rtop.at[c], l_sem.at[10]),
    ]
    for copy in locals_:
        copy.start()

    @pl.when(hub)
    def _():
        for copy in hub_locals:
            copy.start()

    def clear(t, carry):
        acc[t] = jnp.zeros((cols, w), f32)
        return carry

    lax.fori_loop(0, leaf + 6, clear, 0)
    pl.semaphore_wait(barrier, 16)

    def piece(j, k):
        at = pl.ds(j * CHUNK, CHUNK)
        return blk.at[at, :, rows_of[k]], dinv.at[at, rows_of[k]]

    def own(j, to, k, device):
        at = pl.ds(j * CHUNK, CHUNK)
        return [
            remote(lb.at[at], blk.at[at, :, z], s_own.at[to, 0], r_in.at[k, 0, j], device),
            remote(ld.at[at], dinv.at[at, z], s_own.at[to, 1], r_in.at[k, 1, j], device),
        ]

    def onward(j, k, to, into, device):
        b, d = piece(j, k)
        return [
            remote(b, b, s_fwd.at[to, 0], r_in.at[into, 0, j], device),
            remote(d, d, s_fwd.at[to, 1], r_in.at[into, 1, j], device),
        ]

    def arrived(j, k):
        for copy in onward(j, k, 0, k, (sn, zm)):
            copy.wait_recv()

    def rhs_piece(j):
        at = pl.ds(j * CHUNK, CHUNK)
        return remote(rl.at[at], rin.at[at], s_rhs, r_rhs.at[j], (other, zo))

    def send_own(j):
        @pl.when(hub)
        def _():
            for copy in own(j, 0, 2, (sn, zm)) + own(j, 1, 0, (other, z)):
                copy.start()

        @pl.when(guest)
        def _():
            rhs_piece(j).start()
            for copy in own(j, 0, 1, (sn, zo)):
                copy.start()

    send_own(0)

    def top_z(i):
        there = (sn, (zm, zo)[i])
        copies = [remote(td.at[0], tg.at[c, 0, z], s_top.at[i], r_top.at[i], there)]
        for l in range(1, 6):
            copies.append(remote(tb.at[ancestors[l], 0], tg.at[c, l, z], s_top.at[i], r_top.at[i], there))
        return copies

    def top_z_all(i):
        view = tg.at[c, :, (zm, zo, zm)[i]]
        return remote(view, view, s_top.at[i], r_top.at[i], (sn, (zm, zo, zo)[i]))

    for i in range(2):
        for copy in top_z(i):
            copy.start()

    to_guest = remote(st, stv, s_st, r_st, (other, z))

    @pl.when(hub)
    def _():
        to_guest.start()

    def share_rhs(k):
        return remote(rt.at[0, at_cols(k)], rtop.at[c], s_rt.at[k], r_rt.at[c], worker(k))

    def rhs_from(m):
        return remote(rtop.at[m], rtop.at[m], s_rt.at[0], r_rt.at[m], (4 * g + m, zo))

    def not_me(k):
        return jnp.logical_or(guest, place != k)

    def not_own(m):
        return jnp.logical_or(guest, c != m)

    for k in range(4):

        @pl.when(not_me(k))
        def _(k=k):
            share_rhs(k).start()

    for j in range(1, min(AHEAD, chunks)):
        send_own(j)

    def share_group(i):
        what = (c, c, lax.rem(c + 2, 4))[i]
        there = (4 * g + lax.rem(c + 2, 4), other, other)[i]
        return remote(tg.at[what], tg.at[what], s_grp.at[i], r_grp.at[i], (there, z))

    def exists(q, level):
        return (q // (1 << level)) % 2 == 0

    def share_upper(i, slot):
        return remote(
            tg.at[3, slot if slot == 0 else slot + 2], upper.at[g, slot], s_up.at[i, slot], r_up.at[g, slot],
            (classmate(i), z),
        )

    def upper_from(at, slot):
        view = upper.at[at, slot]
        return remote(view, view, s_up.at[0, slot], r_up.at[at, slot], (4 * at + c, z))

    def has_upper(q, slot):
        return jnp.logical_and(exists(q, slot), (q + 1) % (1 << slot) != 0)

    for copy in locals_:
        copy.wait()

    @pl.when(hub)
    def _():
        for copy in hub_locals:
            copy.wait()

    @pl.when(guest)
    def _():
        to_guest.wait_recv()

    into_smem = pltpu.make_async_copy(stv, slot_ref, l_sem.at[11])
    into_smem.start()
    into_smem.wait()

    def slot_of(s, r):
        v = slot_ref[r, s]
        t = v - (leaf - 1)
        level = 0
        for l in range(1, 6):
            level = level + jnp.where((t & ((1 << l) - 1)) == 0, 1, 0)
        return jnp.where(v < leaf, v, leaf + level)

    def leaf_block(s):
        return blk[s].reshape(3 * w, w), dinv[s].reshape(w, w)

    def forward_step(s):
        b, d = leaf_block(s)
        solved = dot3(rin[s] + acc[s], d, True)
        fwd[s] = solved
        out = dot3(solved, b, True)
        acc[s + 1] = acc[s + 1] - out[:, :w]
        first, second = slot_of(s, 1), slot_of(s, 2)
        out1, out2 = out[:, w : 2 * w], out[:, 2 * w :]

        def push(t):
            m1 = (first == t).astype(f32)
            m2 = (second == t).astype(f32)
            acc[t] = acc[t] - (m1 * out1 + m2 * out2)

        for t in range(2, leaf + 6):
            push(t)

    def turn(j, carry):
        @pl.when(j + AHEAD < chunks)
        def _():
            send_own(j + AHEAD)

        @pl.when(hub)
        def _():
            @pl.when(j < chunks)
            def _():
                arrived(j, 1)
                for copy in onward(j, 1, 0, 3, (sn, zm)) + onward(j, 1, 1, 1, (other, z)):
                    copy.start()
                arrived(j, 2)
                for copy in onward(j, 2, 2, 2, (other, z)):
                    copy.start()

            @pl.when(j >= LAG)
            def _():
                arrived(j - LAG, 3)
                for copy in onward(j - LAG, 3, 3, 3, (other, z)):
                    copy.start()

        @pl.when(j == TOP_TURNS[0])
        def _():
            top_z_all(0).wait_recv()
            top_z_all(2).start()

        @pl.when(j == TOP_TURNS[1])
        def _():
            top_z_all(1).wait_recv()
            top_z_all(2).wait()
            column = dot3(tg[c, 1:6].reshape(5 * w, w), tg[c, 0].reshape(w, w), False)
            tg[c, 1:6] = column.reshape(5, 4, quarter, w)

        @pl.when(j == TOP_TURNS[2])
        def _():
            for i in range(2):
                share_group(i).start()

        @pl.when(j == TOP_TURNS[3])
        def _():
            share_group(0).wait_recv()
            share_group(2).start()

        @pl.when(j == TOP_TURNS[4])
        def _():
            share_group(1).wait_recv()
            share_group(2).wait_recv()
            for i in range(1, 8):
                share_upper(i, 0).start()
            for slot in range(1, 4):

                @pl.when(has_upper(g, slot))
                def _(slot=slot):
                    for i in range(1, 8):
                        share_upper(i, slot).start()

        @pl.when(j >= LAG)
        def _():
            @pl.when(guest)
            def _():
                rhs_piece(j - LAG).wait_recv()
                for k in range(4):
                    arrived(j - LAG, k)

            for i in range(CHUNK):
                forward_step((j - LAG) * CHUNK + i)

        return carry

    lax.fori_loop(0, chunks + LAG, turn, 0)

    def share_part(i):
        to, device = mate(place, i)
        return remote(acc.at[pl.ds(leaf, 6), at_cols(to)], part.at[place], s_part.at[i], r_part.at[i], device)

    for i in range(1, 4):
        share_part(i).start()
    part[place] = acc[pl.ds(leaf, 6), my_cols]

    for m in range(4):

        @pl.when(not_own(m))
        def _(m=m):
            rhs_from(m).wait_recv()

    def top_block(m, l):
        return tg[m, l].reshape(w, w)

    def top_stack(m, first=2):
        return tg[m, first:6].reshape((6 - first) * w, w)

    def squared(x, d):
        return dot3(dot3(x, d, True), d, False)

    source2 = rtop[2]
    out2 = dot3(source2, top_stack(2), True)
    upper[g, 0] = tg[3, 0]
    upper[g, 1:4] = tg[3, 3:6]
    for i in range(1, 4):
        share_part(i).wait_recv()
    path = part[0] + part[1] + part[2] + part[3]
    source0 = path[0] + rtop[0]
    out0 = dot3(source0, top_stack(0, 1), True)
    source1 = path[1] + rtop[1] - out0[:, :w]
    out = out0[:, w:] + dot3(source1, top_stack(1), True) + out2
    last = 4 * g + 3
    above = [(last + 1) % (1 << l) == 0 for l in range(6)]
    for l in range(2, 6):
        mine = above[l]
        if l < 5:
            mine = jnp.logical_and(mine, jnp.logical_not(above[l + 1]))
        contrib[l - 2] = path[l] + mine.astype(f32) * rtop[3] - out[:, (l - 2) * w : (l - 1) * w]

    def share_contrib(i, level):
        return remote(
            contrib.at[level], gathered.at[g, level], s_con.at[i, level], r_con.at[g, level], (classmate(i), z)
        )

    def contrib_from(at, level):
        view = gathered.at[at, level]
        return remote(view, view, s_con.at[0, level], r_con.at[at, level], (4 * at + c, z))

    for level in range(4):

        @pl.when(exists(g, level))
        def _(level=level):
            for i in (4, 3, 5, 2, 6, 1, 7):
                share_contrib(i, level).start()

    gathered[g] = contrib[...]
    ftop[0] = squared(source0, top_block(0, 0))
    ftop[1] = squared(source1, top_block(1, 0))
    ftop[2] = squared(source2, top_block(2, 0))
    for i in range(1, 8):
        at = lax.rem(g + i, 8)
        upper_from(at, 0).wait_recv()
        for slot in range(1, 4):

            @pl.when(has_upper(at, slot))
            def _(at=at, slot=slot):
                upper_from(at, slot).wait_recv()

    for i in range(1, 8):
        at = lax.rem(g + i, 8)
        for level in range(4):

            @pl.when(exists(at, level))
            def _(at=at, level=level):
                contrib_from(at, level).wait_recv()

    def upper_block(q, slot):
        return upper[q, slot].reshape(w, w)

    spans = [range(q + 1 - (1 << trailing(q)), q) for q in range(8)]
    order = sorted(range(8), key=lambda q: (trailing(q), q))
    sources, parts = {}, {}
    for q in order:
        level = trailing(q)
        source = gathered[q, level]
        for below in spans[q]:
            source = source + gathered[below, level]
        for below in spans[q]:
            source = source - dot3(sources[below], upper_block(below, level), True)
        sources[q] = source
        parts[q] = squared(source, upper_block(q, 0))
    solved = {}
    for q in reversed(order):
        solved[q] = parts[q]
        for up in range(q + 1, 8):
            if q in spans[up]:
                solved[q] = solved[q] - dot3(solved[up], upper_block(q, trailing(up)), False)
        xs[q] = solved[q]
    for level in range(4):
        q = (g // (1 << level)) * (1 << level) + (1 << level) - 1
        xpath[level] = xs[q] * exists(g, level).astype(f32)

    across = jnp.concatenate([xpath[0], xpath[1], xpath[2], xpath[3]], axis=1)
    x1 = ftop[1] - dot3(across, top_stack(1), False)
    x2 = ftop[2] - dot3(across, top_stack(2), False)
    x0 = ftop[0] - dot3(across, top_stack(0), False) - dot3(x1, top_block(0, 1), False)
    zown[0], zown[1], zown[6] = x0, x1, x2
    zown[2:6] = xpath[...]

    def share_z(i):
        to, device = mate(place, i)
        return remote(zown.at[pl.ds(0, 6)], zbuf.at[pl.ds(leaf, 6), my_cols], s_z.at[i], r_z.at[i], device)

    def z_from(i):
        view = zbuf.at[pl.ds(leaf, 6), at_cols(lax.rem(place + 4 - i, 4))]
        return remote(zown.at[pl.ds(0, 6)], view, s_z.at[i], r_z.at[i], mate(place, i)[1])

    for i in range(1, 4):
        share_z(i).start()
    zbuf[pl.ds(leaf, 6), my_cols] = zown[0:6]

    def level_of(t):
        return sum(jnp.where((t + 1) % (1 << l) == 0, 1, 0) for l in range(1, 6))

    top_slots = (0, 1, 6, level_of(last))

    def share_top(m):
        return remote(zown.at[top_slots[m]], tout.at[my_cols], s_to.at[m], r_to.at[place], (4 * g + m, block))

    def top_from(k):
        return remote(zown.at[0], tout.at[at_cols(k)], s_to.at[0], r_to.at[k], worker(k))

    for m in range(4):

        @pl.when(not_own(m))
        def _(m=m):
            share_top(m).start()

    @pl.when(hub)
    def _():
        tout[my_cols] = zown[jnp.where(c == 2, 6, level_of(sn))]

    for i in range(1, 4):
        z_from(i).wait_recv()

    def back_piece(s):
        return remote(zbuf.at[s], o_leaf.at[s], s_back, r_back, (other, zo))

    def keep_piece(s):
        return pltpu.make_async_copy(zbuf.at[s], o_leaf.at[s], l_sem.at[0])

    def let_go(s):
        @pl.when(hub)
        def _():
            keep_piece(s).start()

        @pl.when(guest)
        def _():
            back_piece(s).start()

    def backward_step(s):
        b, d = leaf_block(s)
        z_at = jnp.concatenate([zbuf[s + 1], zbuf[slot_of(s, 1)], zbuf[slot_of(s, 2)]], axis=1)
        zbuf[s] = dot3(fwd[s] - dot3(z_at, b, False), d, False)

    backward_step(leaf - 1)

    def backward(j, carry):
        s = leaf - 2 - j
        backward_step(s)
        let_go(s + 1)
        return carry

    lax.fori_loop(0, leaf - 1, backward, 0)

    for k in range(4):

        @pl.when(not_me(k))
        def _(k=k):
            top_from(k).wait_recv()

    top_out = pltpu.make_async_copy(tout, o_top.at[0], l_sem.at[1])
    top_out.start()
    let_go(0)

    whole = pl.ds(0, leaf)

    def left(ssem, rows):
        b, d = blk.at[:, :, rows], dinv.at[:, rows]
        remote(b, b, ssem.at[0], r_in.at[0, 0, 0], (sn, zo)).wait_send()
        remote(d, d, ssem.at[1], r_in.at[0, 1, 0], (sn, zo)).wait_send()

    left(s_own.at[0], z)
    for i in range(3):
        if i < 2:
            top_z_all(i).wait_send()
        share_group(i).wait_send()
        share_part(i + 1).wait_send()
        share_z(i + 1).wait_send()
    for m in range(4):

        @pl.when(not_me(m))
        def _(m=m):
            share_rhs(m).wait_send()

        @pl.when(not_own(m))
        def _(m=m):
            share_top(m).wait_send()

    for i in range(1, 8):
        share_upper(i, 0).wait_send()
    for slot in range(1, 4):

        @pl.when(has_upper(g, slot))
        def _(slot=slot):
            for i in range(1, 8):
                share_upper(i, slot).wait_send()

    for level in range(4):

        @pl.when(exists(g, level))
        def _(level=level):
            for i in range(1, 8):
                share_contrib(i, level).wait_send()

    @pl.when(hub)
    def _():
        left(s_own.at[1], z)
        for to in range(4):
            left(s_fwd.at[to], z)
        to_guest.wait_send()
        pltpu.make_async_copy(zbuf.at[whole], o_leaf, l_sem.at[0]).wait()

    @pl.when(guest)
    def _():
        remote(rl, rin, s_rhs, r_rhs.at[0], (other, zo)).wait_send()
        everything = remote(zbuf.at[whole], o_leaf, s_back, r_back, (other, zo))
        everything.wait_send()
        everything.wait_recv()

    top_out.wait()


def local(rl, rt, lb, ld, st, tb, td):
    leaf, cols, w = rl.shape
    cc, quarter, chunks = cols // 4, w // 4, leaf // CHUNK
    any_spec = pl.BlockSpec(memory_space=pl.ANY)
    operands = [pltpu.with_memory_space_constraint(v, pltpu.HBM) for v in (st.T, rl, rt, lb, ld, tb, td)]
    dma = pltpu.SemaphoreType.DMA
    return pl.pallas_call(
        kernel,
        out_shape=(jax.ShapeDtypeStruct(rl.shape, f32), jax.ShapeDtypeStruct(rt.shape, f32)),
        in_specs=[any_spec] * 7,
        out_specs=(pl.BlockSpec(memory_space=pltpu.VMEM),) * 2,
        scratch_shapes=[
            pltpu.VMEM((leaf + 6, cols, w), f32),
            pltpu.VMEM((leaf, cols, w), f32),
            pltpu.VMEM((leaf, 3, 4, quarter, w), f32),
            pltpu.VMEM((leaf, 4, quarter, w), f32),
            pltpu.VMEM((leaf, cols, w), f32),
            pltpu.VMEM((leaf + 6, cols, w), f32),
            pltpu.VMEM((4, 6, 4, quarter, w), f32),
            pltpu.VMEM((4, cc, w), f32),
            pltpu.VMEM((4, 6, cc, w), f32),
            pltpu.VMEM((4, cc, w), f32),
            pltpu.VMEM((8, 4, cc, w), f32),
            pltpu.VMEM((8, 4, 4, quarter, w), f32),
            pltpu.VMEM((8, cc, w), f32),
            pltpu.VMEM((4, cc, w), f32),
            pltpu.VMEM((7, cc, w), f32),
            pltpu.VMEM((3, cc, w), f32),
            pltpu.VMEM((cols, w), f32),
            pltpu.VMEM(st.shape[::-1], jnp.int32),
            pltpu.SMEM(st.shape[::-1], jnp.int32),
            dma((2, 2)), dma((4, 2)), dma, dma, dma((4, 2, chunks)), dma((chunks,)), dma,
            dma((4,)), dma((4,)), dma((4,)), dma((4,)), dma((4,)), dma((4,)),
            dma((8, 4)), dma((8, 4)), dma((4,)), dma((4,)), dma((8, 4)), dma((8, 4)), dma((4,)), dma((4,)),
            dma((4,)), dma((4,)), dma, dma, dma((12,)),
        ],
        compiler_params=pltpu.CompilerParams(
            collective_id=0, has_side_effects=True, vmem_limit_bytes=24*1024*1024
        ),
        name="substitution",
    )(*operands)


def solution(mesh):
    return jax.shard_map(
        local,
        mesh=mesh,
        in_specs=(
            P("sn", "rhs", None),
            P("sn", "rhs", None),
            P("sn", None, "rhs", None),
            P("sn", "rhs", None),
            P("sn", None),
            P(None, "sn", "rhs", None),
            P("sn", "rhs", None),
        ),
        out_specs=(P("sn", "rhs", None), P("sn", "rhs", None)),
        check_vma=False,
    )
```

```python
import functools

import jax
import jax.numpy as jnp
from jax import lax
from jax.experimental import pallas as pl
from jax.experimental.pallas import tpu as pltpu
from jax.sharding import PartitionSpec as P

MESH = pl.DeviceIdType.MESH
f32 = jnp.float32
bf16 = jnp.bfloat16

CHUNK = 2
AHEAD = 3
LAG = 3
TOP_TURNS = 2, 4, 5, 9, 10


def split(x):
    high = x.astype(bf16)
    return high, (x - high.astype(f32)).astype(bf16)


def dot3(x, w, transposed):
    dims = (((1,), (1 if transposed else 0,)), ((), ()))
    dot = functools.partial(lax.dot_general, dimension_numbers=dims, preferred_element_type=f32)
    x_high, x_low = split(x)
    w_high, w_low = split(w)
    m = x.shape[0]
    both = dot(jnp.concatenate([x_high, x_low], axis=0), w_high)
    return both[:m] + (both[m:] + dot(x_high, w_low))


def trailing(q):
    count = 0
    while (q >> count) & 1:
        count += 1
    return count


def kernel(
    st, rl, rt, lb, ld, tb, td,
    o_leaf, o_top,
    acc, rin, blk, dinv, fwd, zbuf, tg, rtop, part, contrib, gathered, upper, xs, xpath, zown, ftop, tout, stv, slot_ref,
    s_own, s_fwd, s_rhs, s_back, r_in, r_rhs, r_back,
    s_top, r_top, s_rt, r_rt, s_grp, r_grp, s_up, r_up, s_part, r_part, s_con, r_con, s_z, r_z, s_to, r_to,
    s_st, r_st, l_sem,
):
    leaf, cols, w = rl.shape
    quarter = w // 4
    cc = cols // 4
    chunks = leaf // CHUNK
    sn, z = lax.axis_index("sn"), lax.axis_index("rhs")
    g, c = sn // 4, sn % 4
    core, low = sn % 2, z // 2
    hub = core == low
    guest = jnp.logical_not(hub)
    role = jnp.where(hub, 0, 1)
    other, zm, zo = sn + 1 - 2 * core, z + 1 - 2 * (z % 2), 3 - z
    rows_of = (z, zo, zm, 3 - zm)
    place = 2 * (c // 2) + role
    block = jnp.where(hub, z, zo)

    def at_cols(k):
        return pl.ds(pl.multiple_of(k * cc, cc), cc)

    my_cols = at_cols(place)

    def sibling(i):
        return 4 * g + lax.rem(c + i, 4)

    def classmate(i):
        return 4 * lax.rem(g + i, 8) + c

    def mate(k, i):
        dy, dr = ((1, 1), (1, 0), (0, 1))[i - 1]
        to = 2 * ((c // 2 + dy) % 2) + (role + dr) % 2
        return to, (4 * g + 2 * (to // 2) + core, jnp.where(to % 2 == role, z, zo))

    def worker(k):
        return 4 * g + 2 * (k // 2) + low, (z if k % 2 == 0 else zo)

    def remote(src, dst, ssem, rsem, device):
        return pltpu.make_async_remote_copy(
            src_ref=src, dst_ref=dst, send_sem=ssem, recv_sem=rsem, device_id=device, device_id_type=MESH
        )

    barrier = pltpu.get_barrier_semaphore()

    def greet(device):
        pl.semaphore_signal(barrier, inc=1, device_id=device, device_id_type=MESH)

    for i in range(1, 4):
        greet((sibling(i), z))
    for i in range(4):
        greet((sibling(i), zo))
    greet((sn, zm))
    greet((sn, 3 - zm))
    for i in range(1, 8):
        greet((classmate(i), z))

    locals_ = [pltpu.make_async_copy(td.at[0], tg.at[c, 0, z], l_sem.at[0])]
    ancestors = [(sn >> l) * (1 << l) + ((1 << l) - 1) for l in range(6)]
    for l in range(1, 6):
        locals_.append(pltpu.make_async_copy(tb.at[ancestors[l], 0], tg.at[c, l, z], l_sem.at[l]))
    hub_locals = [
        pltpu.make_async_copy(rl, rin, l_sem.at[6]),
        pltpu.make_async_copy(lb, blk.at[:, :, z], l_sem.at[7]),
        pltpu.make_async_copy(ld, dinv.at[:, z], l_sem.at[8]),
        pltpu.make_async_copy(st, stv, l_sem.at[9]),
        pltpu.make_async_copy(rt.at[0, my_cols], rtop.at[c], l_sem.at[10]),
    ]
    for copy in locals_:
        copy.start()

    @pl.when(hub)
    def _():
        for copy in hub_locals:
            copy.start()

    def clear(t, carry):
        acc[t] = jnp.zeros((cols, w), f32)
        return carry

    lax.fori_loop(0, leaf + 6, clear, 0)
    pl.semaphore_wait(barrier, 16)

    def piece(j, k):
        at = pl.ds(j * CHUNK, CHUNK)
        return blk.at[at, :, rows_of[k]], dinv.at[at, rows_of[k]]

    def own(j, to, k, device):
        at = pl.ds(j * CHUNK, CHUNK)
        return [
            remote(lb.at[at], blk.at[at, :, z], s_own.at[to, 0], r_in.at[k, 0, j], device),
            remote(ld.at[at], dinv.at[at, z], s_own.at[to, 1], r_in.at[k, 1, j], device),
        ]

    def onward(j, k, to, into, device):
        b, d = piece(j, k)
        return [
            remote(b, b, s_fwd.at[to, 0], r_in.at[into, 0, j], device),
            remote(d, d, s_fwd.at[to, 1], r_in.at[into, 1, j], device),
        ]

    def arrived(j, k):
        for copy in onward(j, k, 0, k, (sn, zm)):
            copy.wait_recv()

    def rhs_piece(j):
        at = pl.ds(j * CHUNK, CHUNK)
        return remote(rl.at[at], rin.at[at], s_rhs, r_rhs.at[j], (other, zo))

    def send_own(j):
        @pl.when(hub)
        def _():
            for copy in own(j, 0, 2, (sn, zm)) + own(j, 1, 0, (other, z)):
                copy.start()

        @pl.when(guest)
        def _():
            rhs_piece(j).start()
            for copy in own(j, 0, 1, (sn, zo)):
                copy.start()

    send_own(0)

    def top_z(i):
        there = (sn, (zm, zo)[i])
        copies = [remote(td.at[0], tg.at[c, 0, z], s_top.at[i], r_top.at[i], there)]
        for l in range(1, 6):
            copies.append(remote(tb.at[ancestors[l], 0], tg.at[c, l, z], s_top.at[i], r_top.at[i], there))
        return copies

    def top_z_all(i):
        view = tg.at[c, :, (zm, zo, zm)[i]]
        return remote(view, view, s_top.at[i], r_top.at[i], (sn, (zm, zo, zo)[i]))

    for i in range(2):
        for copy in top_z(i):
            copy.start()

    to_guest = remote(st, stv, s_st, r_st, (other, z))

    @pl.when(hub)
    def _():
        to_guest.start()

    def share_rhs(k):
        return remote(rt.at[0, at_cols(k)], rtop.at[c], s_rt.at[k], r_rt.at[c], worker(k))

    def rhs_from(m):
        return remote(rtop.at[m], rtop.at[m], s_rt.at[0], r_rt.at[m], (4 * g + m, zo))

    def not_me(k):
        return jnp.logical_or(guest, place != k)

    def not_own(m):
        return jnp.logical_or(guest, c != m)

    for k in range(4):

        @pl.when(not_me(k))
        def _(k=k):
            share_rhs(k).start()

    for j in range(1, min(AHEAD, chunks)):
        send_own(j)

    def share_group(i):
        what = (c, c, lax.rem(c + 2, 4))[i]
        there = (4 * g + lax.rem(c + 2, 4), other, other)[i]
        return remote(tg.at[what], tg.at[what], s_grp.at[i], r_grp.at[i], (there, z))

    def exists(q, level):
        return (q // (1 << level)) % 2 == 0

    def share_upper(i, slot):
        return remote(
            tg.at[3, slot if slot == 0 else slot + 2], upper.at[g, slot], s_up.at[i, slot], r_up.at[g, slot],
            (classmate(i), z),
        )

    def upper_from(at, slot):
        view = upper.at[at, slot]
        return remote(view, view, s_up.at[0, slot], r_up.at[at, slot], (4 * at + c, z))

    def has_upper(q, slot):
        return jnp.logical_and(exists(q, slot), (q + 1) % (1 << slot) != 0)

    for copy in locals_:
        copy.wait()

    @pl.when(hub)
    def _():
        for copy in hub_locals:
            copy.wait()

    @pl.when(guest)
    def _():
        to_guest.wait_recv()

    into_smem = pltpu.make_async_copy(stv, slot_ref, l_sem.at[11])
    into_smem.start()
    into_smem.wait()

    def slot_of(s, r):
        v = slot_ref[r, s]
        t = v - (leaf - 1)
        level = 0
        for l in range(1, 6):
            level = level + jnp.where((t & ((1 << l) - 1)) == 0, 1, 0)
        return jnp.where(v < leaf, v, leaf + level)

    def leaf_block(s):
        return blk[s].reshape(3 * w, w), dinv[s].reshape(w, w)

    def forward_step(s):
        b, d = leaf_block(s)
        solved = dot3(rin[s] + acc[s], d, True)
        fwd[s] = solved
        out = dot3(solved, b, True)
        acc[s + 1] = acc[s + 1] - out[:, :w]
        first, second = slot_of(s, 1), slot_of(s, 2)
        out1, out2 = out[:, w : 2 * w], out[:, 2 * w :]

        def push(t):
            m1 = (first == t).astype(f32)
            m2 = (second == t).astype(f32)
            acc[t] = acc[t] - (m1 * out1 + m2 * out2)

        for start in range(0, leaf, 8):

            @pl.when(s + 2 < min(start + 8, leaf))
            def _(start=start):
                for t in range(max(start, 2), min(start + 8, leaf)):
                    push(t)

        for t in range(leaf, leaf + 6):
            push(t)

    def turn(j, carry):
        @pl.when(j + AHEAD < chunks)
        def _():
            send_own(j + AHEAD)

        @pl.when(hub)
        def _():
            @pl.when(j < chunks)
            def _():
                arrived(j, 1)
                for copy in onward(j, 1, 0, 3, (sn, zm)) + onward(j, 1, 1, 1, (other, z)):
                    copy.start()
                arrived(j, 2)
                for copy in onward(j, 2, 2, 2, (other, z)):
                    copy.start()

            @pl.when(j >= LAG)
            def _():
                arrived(j - LAG, 3)
                for copy in onward(j - LAG, 3, 3, 3, (other, z)):
                    copy.start()

        @pl.when(j == TOP_TURNS[0])
        def _():
            top_z_all(0).wait_recv()
            top_z_all(2).start()

        @pl.when(j == TOP_TURNS[1])
        def _():
            top_z_all(1).wait_recv()
            top_z_all(2).wait()
            column = dot3(tg[c, 1:6].reshape(5 * w, w), tg[c, 0].reshape(w, w), False)
            tg[c, 1:6] = column.reshape(5, 4, quarter, w)

        @pl.when(j == TOP_TURNS[2])
        def _():
            for i in range(2):
                share_group(i).start()

        @pl.when(j == TOP_TURNS[3])
        def _():
            share_group(0).wait_recv()
            share_group(2).start()

        @pl.when(j == TOP_TURNS[4])
        def _():
            share_group(1).wait_recv()
            share_group(2).wait_recv()
            for i in range(1, 8):
                share_upper(i, 0).start()
            for slot in range(1, 4):

                @pl.when(has_upper(g, slot))
                def _(slot=slot):
                    for i in range(1, 8):
                        share_upper(i, slot).start()

        @pl.when(j >= LAG)
        def _():
            @pl.when(guest)
            def _():
                rhs_piece(j - LAG).wait_recv()
                for k in range(4):
                    arrived(j - LAG, k)

            for i in range(CHUNK):
                forward_step((j - LAG) * CHUNK + i)

        return carry

    lax.fori_loop(0, chunks + LAG, turn, 0)

    def share_part(i):
        to, device = mate(place, i)
        return remote(acc.at[pl.ds(leaf, 6), at_cols(to)], part.at[place], s_part.at[i], r_part.at[i], device)

    for i in range(1, 4):
        share_part(i).start()
    part[place] = acc[pl.ds(leaf, 6), my_cols]

    for m in range(4):

        @pl.when(not_own(m))
        def _(m=m):
            rhs_from(m).wait_recv()

    def top_block(m, l):
        return tg[m, l].reshape(w, w)

    def top_stack(m, first=2):
        return tg[m, first:6].reshape((6 - first) * w, w)

    def squared(x, d):
        return dot3(dot3(x, d, True), d, False)

    source2 = rtop[2]
    out2 = dot3(source2, top_stack(2), True)
    upper[g, 0] = tg[3, 0]
    upper[g, 1:4] = tg[3, 3:6]
    for i in range(1, 4):
        share_part(i).wait_recv()
    path = part[0] + part[1] + part[2] + part[3]
    source0 = path[0] + rtop[0]
    out0 = dot3(source0, top_stack(0, 1), True)
    source1 = path[1] + rtop[1] - out0[:, :w]
    out = out0[:, w:] + dot3(source1, top_stack(1), True) + out2
    last = 4 * g + 3
    above = [(last + 1) % (1 << l) == 0 for l in range(6)]
    for l in range(2, 6):
        mine = above[l]
        if l < 5:
            mine = jnp.logical_and(mine, jnp.logical_not(above[l + 1]))
        contrib[l - 2] = path[l] + mine.astype(f32) * rtop[3] - out[:, (l - 2) * w : (l - 1) * w]

    def share_contrib(i, level):
        return remote(
            contrib.at[level], gathered.at[g, level], s_con.at[i, level], r_con.at[g, level], (classmate(i), z)
        )

    def contrib_from(at, level):
        view = gathered.at[at, level]
        return remote(view, view, s_con.at[0, level], r_con.at[at, level], (4 * at + c, z))

    for level in range(4):

        @pl.when(exists(g, level))
        def _(level=level):
            for i in (4, 3, 5, 2, 6, 1, 7):
                share_contrib(i, level).start()

    gathered[g] = contrib[...]
    ftop[0] = squared(source0, top_block(0, 0))
    ftop[1] = squared(source1, top_block(1, 0))
    ftop[2] = squared(source2, top_block(2, 0))
    for i in range(1, 8):
        at = lax.rem(g + i, 8)
        upper_from(at, 0).wait_recv()
        for slot in range(1, 4):

            @pl.when(has_upper(at, slot))
            def _(at=at, slot=slot):
                upper_from(at, slot).wait_recv()

    for i in range(1, 8):
        at = lax.rem(g + i, 8)
        for level in range(4):

            @pl.when(exists(at, level))
            def _(at=at, level=level):
                contrib_from(at, level).wait_recv()

    def upper_block(q, slot):
        return upper[q, slot].reshape(w, w)

    spans = [range(q + 1 - (1 << trailing(q)), q) for q in range(8)]
    order = sorted(range(8), key=lambda q: (trailing(q), q))
    sources, parts = {}, {}
    for q in order:
        level = trailing(q)
        source = gathered[q, level]
        for below in spans[q]:
            source = source + gathered[below, level]
        for below in spans[q]:
            source = source - dot3(sources[below], upper_block(below, level), True)
        sources[q] = source
        parts[q] = squared(source, upper_block(q, 0))
    solved = {}
    for q in reversed(order):
        solved[q] = parts[q]
        for up in range(q + 1, 8):
            if q in spans[up]:
                solved[q] = solved[q] - dot3(solved[up], upper_block(q, trailing(up)), False)
        xs[q] = solved[q]
    for level in range(4):
        q = (g // (1 << level)) * (1 << level) + (1 << level) - 1
        xpath[level] = xs[q] * exists(g, level).astype(f32)

    across = jnp.concatenate([xpath[0], xpath[1], xpath[2], xpath[3]], axis=1)
    x1 = ftop[1] - dot3(across, top_stack(1), False)
    x2 = ftop[2] - dot3(across, top_stack(2), False)
    x0 = ftop[0] - dot3(across, top_stack(0), False) - dot3(x1, top_block(0, 1), False)
    zown[0], zown[1], zown[6] = x0, x1, x2
    zown[2:6] = xpath[...]

    def share_z(i):
        to, device = mate(place, i)
        return remote(zown.at[pl.ds(0, 6)], zbuf.at[pl.ds(leaf, 6), my_cols], s_z.at[i], r_z.at[i], device)

    def z_from(i):
        view = zbuf.at[pl.ds(leaf, 6), at_cols(mate(place, i)[0])]
        return remote(zown.at[pl.ds(0, 6)], view, s_z.at[i], r_z.at[i], mate(place, i)[1])

    for i in range(1, 4):
        share_z(i).start()
    zbuf[pl.ds(leaf, 6), my_cols] = zown[0:6]

    def level_of(t):
        return sum(jnp.where((t + 1) % (1 << l) == 0, 1, 0) for l in range(1, 6))

    top_slots = (0, 1, 6, level_of(last))

    def share_top(m):
        return remote(zown.at[top_slots[m]], tout.at[my_cols], s_to.at[m], r_to.at[place], (4 * g + m, block))

    def top_from(k):
        return remote(zown.at[0], tout.at[at_cols(k)], s_to.at[0], r_to.at[k], worker(k))

    for m in range(4):

        @pl.when(not_own(m))
        def _(m=m):
            share_top(m).start()

    @pl.when(hub)
    def _():
        tout[my_cols] = zown[jnp.where(c == 2, 6, level_of(sn))]

    for i in range(1, 4):
        z_from(i).wait_recv()

    def back_piece(s):
        return remote(zbuf.at[s], o_leaf.at[s], s_back, r_back, (other, zo))

    def keep_piece(s):
        return pltpu.make_async_copy(zbuf.at[s], o_leaf.at[s], l_sem.at[0])

    def let_go(s):
        @pl.when(hub)
        def _():
            keep_piece(s).start()

        @pl.when(guest)
        def _():
            back_piece(s).start()

    def backward_step(s):
        b, d = leaf_block(s)
        z_at = jnp.concatenate([zbuf[s + 1], zbuf[slot_of(s, 1)], zbuf[slot_of(s, 2)]], axis=1)
        zbuf[s] = dot3(fwd[s] - dot3(z_at, b, False), d, False)

    backward_step(leaf - 1)

    def backward(j, carry):
        s = leaf - 2 - j
        backward_step(s)
        let_go(s + 1)
        return carry

    lax.fori_loop(0, leaf - 1, backward, 0)

    for k in range(4):

        @pl.when(not_me(k))
        def _(k=k):
            top_from(k).wait_recv()

    top_out = pltpu.make_async_copy(tout, o_top.at[0], l_sem.at[1])
    top_out.start()
    let_go(0)

    whole = pl.ds(0, leaf)

    def left(ssem, rows):
        b, d = blk.at[:, :, rows], dinv.at[:, rows]
        remote(b, b, ssem.at[0], r_in.at[0, 0, 0], (sn, zo)).wait_send()
        remote(d, d, ssem.at[1], r_in.at[0, 1, 0], (sn, zo)).wait_send()

    left(s_own.at[0], z)
    for i in range(3):
        if i < 2:
            top_z_all(i).wait_send()
        share_group(i).wait_send()
        share_part(i + 1).wait_send()
        share_z(i + 1).wait_send()
    for m in range(4):

        @pl.when(not_me(m))
        def _(m=m):
            share_rhs(m).wait_send()

        @pl.when(not_own(m))
        def _(m=m):
            share_top(m).wait_send()

    for i in range(1, 8):
        share_upper(i, 0).wait_send()
    for slot in range(1, 4):

        @pl.when(has_upper(g, slot))
        def _(slot=slot):
            for i in range(1, 8):
                share_upper(i, slot).wait_send()

    for level in range(4):

        @pl.when(exists(g, level))
        def _(level=level):
            for i in range(1, 8):
                share_contrib(i, level).wait_send()

    @pl.when(hub)
    def _():
        left(s_own.at[1], z)
        for to in range(4):
            left(s_fwd.at[to], z)
        to_guest.wait_send()
        pltpu.make_async_copy(zbuf.at[whole], o_leaf, l_sem.at[0]).wait()

    @pl.when(guest)
    def _():
        remote(rl, rin, s_rhs, r_rhs.at[0], (other, zo)).wait_send()
        everything = remote(zbuf.at[whole], o_leaf, s_back, r_back, (other, zo))
        everything.wait_send()
        everything.wait_recv()

    top_out.wait()


def local(rl, rt, lb, ld, st, tb, td):
    leaf, cols, w = rl.shape
    cc, quarter, chunks = cols // 4, w // 4, leaf // CHUNK
    any_spec = pl.BlockSpec(memory_space=pl.ANY)
    operands = [pltpu.with_memory_space_constraint(v, pltpu.HBM) for v in (st.T, rl, rt, lb, ld, tb, td)]
    dma = pltpu.SemaphoreType.DMA
    return pl.pallas_call(
        kernel,
        out_shape=(jax.ShapeDtypeStruct(rl.shape, f32), jax.ShapeDtypeStruct(rt.shape, f32)),
        in_specs=[any_spec] * 7,
        out_specs=(pl.BlockSpec(memory_space=pltpu.VMEM),) * 2,
        scratch_shapes=[
            pltpu.VMEM((leaf + 6, cols, w), f32),
            pltpu.VMEM((leaf, cols, w), f32),
            pltpu.VMEM((leaf, 3, 4, quarter, w), f32),
            pltpu.VMEM((leaf, 4, quarter, w), f32),
            pltpu.VMEM((leaf, cols, w), f32),
            pltpu.VMEM((leaf + 6, cols, w), f32),
            pltpu.VMEM((4, 6, 4, quarter, w), f32),
            pltpu.VMEM((4, cc, w), f32),
            pltpu.VMEM((4, 6, cc, w), f32),
            pltpu.VMEM((4, cc, w), f32),
            pltpu.VMEM((8, 4, cc, w), f32),
            pltpu.VMEM((8, 4, 4, quarter, w), f32),
            pltpu.VMEM((8, cc, w), f32),
            pltpu.VMEM((4, cc, w), f32),
            pltpu.VMEM((7, cc, w), f32),
            pltpu.VMEM((3, cc, w), f32),
            pltpu.VMEM((cols, w), f32),
            pltpu.VMEM(st.shape[::-1], jnp.int32),
            pltpu.SMEM(st.shape[::-1], jnp.int32),
            dma((2, 2)), dma((4, 2)), dma, dma, dma((4, 2, chunks)), dma((chunks,)), dma,
            dma((4,)), dma((4,)), dma((4,)), dma((4,)), dma((4,)), dma((4,)),
            dma((8, 4)), dma((8, 4)), dma((4,)), dma((4,)), dma((8, 4)), dma((8, 4)), dma((4,)), dma((4,)),
            dma((4,)), dma((4,)), dma, dma, dma((12,)),
        ],
        compiler_params=pltpu.CompilerParams(
            collective_id=0, has_side_effects=True, vmem_limit_bytes=24*1024*1024
        ),
        name="substitution",
    )(*operands)


def solution(mesh):
    return jax.shard_map(
        local,
        mesh=mesh,
        in_specs=(
            P("sn", "rhs", None),
            P("sn", "rhs", None),
            P("sn", None, "rhs", None),
            P("sn", "rhs", None),
            P("sn", None),
            P(None, "sn", "rhs", None),
            P("sn", "rhs", None),
        ),
        out_specs=(P("sn", "rhs", None), P("sn", "rhs", None)),
        check_vma=False,
    )
```

```python
import functools

import jax
import jax.numpy as jnp
from jax import lax
from jax.experimental import pallas as pl
from jax.experimental.pallas import tpu as pltpu
from jax.sharding import PartitionSpec as P

MESH = pl.DeviceIdType.MESH
f32 = jnp.float32
bf16 = jnp.bfloat16

CHUNK = 2
AHEAD = 3
LAG = 3
TOP_TURNS = 2, 4, 5, 9, 10


def split(x):
    high = x.astype(bf16)
    return high, (x - high.astype(f32)).astype(bf16)


def dot3(x, w, transposed):
    dims = (((1,), (1 if transposed else 0,)), ((), ()))
    dot = functools.partial(lax.dot_general, dimension_numbers=dims, preferred_element_type=f32)
    x_high, x_low = split(x)
    w_high, w_low = split(w)
    m = x.shape[0]
    both = dot(jnp.concatenate([x_high, x_low], axis=0), w_high)
    return both[:m] + (both[m:] + dot(x_high, w_low))


def trailing(q):
    count = 0
    while (q >> count) & 1:
        count += 1
    return count


def kernel(
    st, rl, rt, lb, ld, tb, td,
    o_leaf, o_top,
    acc, rin, blk, dinv, fwd, zbuf, tg, rtop, part, contrib, gathered, upper, xs, xpath, zown, ftop, tout, stv, slot_ref,
    s_own, s_fwd, s_rhs, s_back, r_in, r_rhs, r_back,
    s_top, r_top, s_rt, r_rt, s_grp, r_grp, s_up, r_up, s_part, r_part, s_con, r_con, s_z, r_z, s_to, r_to,
    s_st, r_st, l_sem,
):
    leaf, cols, w = rl.shape
    quarter = w // 4
    cc = cols // 4
    chunks = leaf // CHUNK
    sn, z = lax.axis_index("sn"), lax.axis_index("rhs")
    g, c = sn // 4, sn % 4
    core, low = sn % 2, z // 2
    hub = core == low
    guest = jnp.logical_not(hub)
    role = jnp.where(hub, 0, 1)
    other, zm, zo = sn + 1 - 2 * core, z + 1 - 2 * (z % 2), 3 - z
    rows_of = (z, zo, zm, 3 - zm)
    place = 2 * (c // 2) + role
    block = jnp.where(hub, z, zo)

    def at_cols(k):
        return pl.ds(pl.multiple_of(k * cc, cc), cc)

    my_cols = at_cols(place)

    def sibling(i):
        return 4 * g + lax.rem(c + i, 4)

    def classmate(i):
        return 4 * lax.rem(g + i, 8) + c

    def mate(k, i):
        dy, dr = ((1, 1), (1, 0), (0, 1))[i - 1]
        to = 2 * ((c // 2 + dy) % 2) + (role + dr) % 2
        return to, (4 * g + 2 * (to // 2) + core, jnp.where(to % 2 == role, z, zo))

    def worker(k):
        return 4 * g + 2 * (k // 2) + low, (z if k % 2 == 0 else zo)

    def remote(src, dst, ssem, rsem, device):
        return pltpu.make_async_remote_copy(
            src_ref=src, dst_ref=dst, send_sem=ssem, recv_sem=rsem, device_id=device, device_id_type=MESH
        )

    barrier = pltpu.get_barrier_semaphore()

    def greet(device):
        pl.semaphore_signal(barrier, inc=1, device_id=device, device_id_type=MESH)

    for i in range(1, 4):
        greet((sibling(i), z))
    for i in range(4):
        greet((sibling(i), zo))
    greet((sn, zm))
    greet((sn, 3 - zm))
    for i in range(1, 8):
        greet((classmate(i), z))

    locals_ = [pltpu.make_async_copy(td.at[0], tg.at[c, 0, z], l_sem.at[0])]
    ancestors = [(sn >> l) * (1 << l) + ((1 << l) - 1) for l in range(6)]
    for l in range(1, 6):
        locals_.append(pltpu.make_async_copy(tb.at[ancestors[l], 0], tg.at[c, l, z], l_sem.at[l]))
    hub_locals = [
        pltpu.make_async_copy(rl, rin, l_sem.at[6]),
        pltpu.make_async_copy(lb, blk.at[:, :, z], l_sem.at[7]),
        pltpu.make_async_copy(ld, dinv.at[:, z], l_sem.at[8]),
        pltpu.make_async_copy(st, stv, l_sem.at[9]),
        pltpu.make_async_copy(rt.at[0, my_cols], rtop.at[c], l_sem.at[10]),
    ]
    for copy in locals_:
        copy.start()

    @pl.when(hub)
    def _():
        for copy in hub_locals:
            copy.start()

    def clear(t, carry):
        acc[t] = jnp.zeros((cols, w), f32)
        return carry

    lax.fori_loop(0, leaf + 6, clear, 0)
    pl.semaphore_wait(barrier, 16)

    def piece(j, k):
        at = pl.ds(j * CHUNK, CHUNK)
        return blk.at[at, :, rows_of[k]], dinv.at[at, rows_of[k]]

    def own(j, to, k, device):
        at = pl.ds(j * CHUNK, CHUNK)
        return [
            remote(lb.at[at], blk.at[at, :, z], s_own.at[to, 0], r_in.at[k, 0, j], device),
            remote(ld.at[at], dinv.at[at, z], s_own.at[to, 1], r_in.at[k, 1, j], device),
        ]

    def onward(j, k, to, into, device):
        b, d = piece(j, k)
        return [
            remote(b, b, s_fwd.at[to, 0], r_in.at[into, 0, j], device),
            remote(d, d, s_fwd.at[to, 1], r_in.at[into, 1, j], device),
        ]

    def arrived(j, k):
        for copy in onward(j, k, 0, k, (sn, zm)):
            copy.wait_recv()

    def rhs_piece(j):
        at = pl.ds(j * CHUNK, CHUNK)
        return remote(rl.at[at], rin.at[at], s_rhs, r_rhs.at[j], (other, zo))

    def send_own(j):
        @pl.when(hub)
        def _():
            for copy in own(j, 0, 2, (sn, zm)) + own(j, 1, 0, (other, z)):
                copy.start()

        @pl.when(guest)
        def _():
            for copy in own(j, 0, 1, (sn, zo)):
                copy.start()
            rhs_piece(j).start()

    send_own(0)

    def top_z(i):
        there = (sn, (zm, zo)[i])
        copies = [remote(td.at[0], tg.at[c, 0, z], s_top.at[i], r_top.at[i], there)]
        for l in range(1, 6):
            copies.append(remote(tb.at[ancestors[l], 0], tg.at[c, l, z], s_top.at[i], r_top.at[i], there))
        return copies

    def top_z_all(i):
        view = tg.at[c, :, (zm, zo, zm)[i]]
        return remote(view, view, s_top.at[i], r_top.at[i], (sn, (zm, zo, zo)[i]))

    for i in range(2):
        for copy in top_z(i):
            copy.start()

    to_guest = remote(st, stv, s_st, r_st, (other, z))

    @pl.when(hub)
    def _():
        to_guest.start()

    def share_rhs(k):
        return remote(rt.at[0, at_cols(k)], rtop.at[c], s_rt.at[k], r_rt.at[c], worker(k))

    def rhs_from(m):
        return remote(rtop.at[m], rtop.at[m], s_rt.at[0], r_rt.at[m], (4 * g + m, zo))

    def not_me(k):
        return jnp.logical_or(guest, place != k)

    def not_own(m):
        return jnp.logical_or(guest, c != m)

    for k in range(4):

        @pl.when(not_me(k))
        def _(k=k):
            share_rhs(k).start()

    for j in range(1, min(AHEAD, chunks)):
        send_own(j)

    def share_group(i):
        what = (c, c, lax.rem(c + 2, 4))[i]
        there = (4 * g + lax.rem(c + 2, 4), other, other)[i]
        return remote(tg.at[what], tg.at[what], s_grp.at[i], r_grp.at[i], (there, z))

    def exists(q, level):
        return (q // (1 << level)) % 2 == 0

    def share_upper(i, slot):
        return remote(
            tg.at[3, slot if slot == 0 else slot + 2], upper.at[g, slot], s_up.at[i, slot], r_up.at[g, slot],
            (classmate(i), z),
        )

    def upper_from(at, slot):
        view = upper.at[at, slot]
        return remote(view, view, s_up.at[0, slot], r_up.at[at, slot], (4 * at + c, z))

    def has_upper(q, slot):
        return jnp.logical_and(exists(q, slot), (q + 1) % (1 << slot) != 0)

    for copy in locals_:
        copy.wait()

    @pl.when(hub)
    def _():
        for copy in hub_locals:
            copy.wait()

    @pl.when(guest)
    def _():
        to_guest.wait_recv()

    into_smem = pltpu.make_async_copy(stv, slot_ref, l_sem.at[11])
    into_smem.start()
    into_smem.wait()

    def slot_of(s, r):
        v = slot_ref[r, s]
        t = v - (leaf - 1)
        level = 0
        for l in range(1, 6):
            level = level + jnp.where((t & ((1 << l) - 1)) == 0, 1, 0)
        return jnp.where(v < leaf, v, leaf + level)

    def leaf_block(s):
        return blk[s].reshape(3 * w, w), dinv[s].reshape(w, w)

    def forward_step(s):
        b, d = leaf_block(s)
        solved = dot3(rin[s] + acc[s], d, True)
        fwd[s] = solved
        out = dot3(solved, b, True)
        acc[s + 1] = acc[s + 1] - out[:, :w]
        first, second = slot_of(s, 1), slot_of(s, 2)
        out1, out2 = out[:, w : 2 * w], out[:, 2 * w :]

        def push(t):
            m1 = (first == t).astype(f32)
            m2 = (second == t).astype(f32)
            acc[t] = acc[t] - (m1 * out1 + m2 * out2)

        for start in range(0, leaf, 8):

            @pl.when(s + 2 < min(start + 8, leaf))
            def _(start=start):
                for t in range(max(start, 2), min(start + 8, leaf)):
                    push(t)

        for t in range(leaf, leaf + 6):
            push(t)

    def turn(j, carry):
        @pl.when(j + AHEAD < chunks)
        def _():
            send_own(j + AHEAD)

        @pl.when(hub)
        def _():
            @pl.when(j < chunks)
            def _():
                arrived(j, 1)
                for copy in onward(j, 1, 0, 3, (sn, zm)) + onward(j, 1, 1, 1, (other, z)):
                    copy.start()
                arrived(j, 2)
                for copy in onward(j, 2, 2, 2, (other, z)):
                    copy.start()

            @pl.when(j >= LAG)
            def _():
                arrived(j - LAG, 3)
                for copy in onward(j - LAG, 3, 3, 3, (other, z)):
                    copy.start()

        @pl.when(j == TOP_TURNS[0])
        def _():
            top_z_all(0).wait_recv()
            top_z_all(2).start()

        @pl.when(j == TOP_TURNS[1])
        def _():
            top_z_all(1).wait_recv()
            top_z_all(2).wait()
            column = dot3(tg[c, 1:6].reshape(5 * w, w), tg[c, 0].reshape(w, w), False)
            tg[c, 1:6] = column.reshape(5, 4, quarter, w)

        @pl.when(j == TOP_TURNS[2])
        def _():
            for i in range(2):
                share_group(i).start()

        @pl.when(j == TOP_TURNS[3])
        def _():
            share_group(0).wait_recv()
            share_group(2).start()

        @pl.when(j == TOP_TURNS[4])
        def _():
            share_group(1).wait_recv()
            share_group(2).wait_recv()
            for i in range(1, 8):
                share_upper(i, 0).start()
            for slot in range(1, 4):

                @pl.when(has_upper(g, slot))
                def _(slot=slot):
                    for i in range(1, 8):
                        share_upper(i, slot).start()

        @pl.when(j >= LAG)
        def _():
            @pl.when(guest)
            def _():
                rhs_piece(j - LAG).wait_recv()
                for k in range(4):
                    arrived(j - LAG, k)

            for i in range(CHUNK):
                forward_step((j - LAG) * CHUNK + i)

        return carry

    lax.fori_loop(0, chunks + LAG, turn, 0)

    def share_part(i):
        to, device = mate(place, i)
        return remote(acc.at[pl.ds(leaf, 6), at_cols(to)], part.at[place], s_part.at[i], r_part.at[i], device)

    for i in range(1, 4):
        share_part(i).start()
    part[place] = acc[pl.ds(leaf, 6), my_cols]

    for m in range(4):

        @pl.when(not_own(m))
        def _(m=m):
            rhs_from(m).wait_recv()

    def top_block(m, l):
        return tg[m, l].reshape(w, w)

    def top_stack(m, first=2):
        return tg[m, first:6].reshape((6 - first) * w, w)

    def squared(x, d):
        return dot3(dot3(x, d, True), d, False)

    source2 = rtop[2]
    out2 = dot3(source2, top_stack(2), True)
    upper[g, 0] = tg[3, 0]
    upper[g, 1:4] = tg[3, 3:6]
    for i in range(1, 4):
        share_part(i).wait_recv()
    path = part[0] + part[1] + part[2] + part[3]
    source0 = path[0] + rtop[0]
    out0 = dot3(source0, top_stack(0, 1), True)
    source1 = path[1] + rtop[1] - out0[:, :w]
    out = out0[:, w:] + dot3(source1, top_stack(1), True) + out2
    last = 4 * g + 3
    above = [(last + 1) % (1 << l) == 0 for l in range(6)]
    for l in range(2, 6):
        mine = above[l]
        if l < 5:
            mine = jnp.logical_and(mine, jnp.logical_not(above[l + 1]))
        contrib[l - 2] = path[l] + mine.astype(f32) * rtop[3] - out[:, (l - 2) * w : (l - 1) * w]

    def share_contrib(i, level):
        return remote(
            contrib.at[level], gathered.at[g, level], s_con.at[i, level], r_con.at[g, level], (classmate(i), z)
        )

    def contrib_from(at, level):
        view = gathered.at[at, level]
        return remote(view, view, s_con.at[0, level], r_con.at[at, level], (4 * at + c, z))

    for i in (5, 3, 4, 2, 6, 1, 7):
        for level in range(4):

            @pl.when(exists(g, level))
            def _(i=i, level=level):
                share_contrib(i, level).start()

    gathered[g] = contrib[...]
    ftop[0] = squared(source0, top_block(0, 0))
    ftop[1] = squared(source1, top_block(1, 0))
    ftop[2] = squared(source2, top_block(2, 0))
    for i in range(1, 8):
        at = lax.rem(g + i, 8)
        upper_from(at, 0).wait_recv()
        for slot in range(1, 4):

            @pl.when(has_upper(at, slot))
            def _(at=at, slot=slot):
                upper_from(at, slot).wait_recv()

    for i in range(1, 8):
        at = lax.rem(g + i, 8)
        for level in range(4):

            @pl.when(exists(at, level))
            def _(at=at, level=level):
                contrib_from(at, level).wait_recv()

    def upper_block(q, slot):
        return upper[q, slot].reshape(w, w)

    spans = [range(q + 1 - (1 << trailing(q)), q) for q in range(8)]
    order = sorted(range(8), key=lambda q: (trailing(q), q))
    sources, parts = {}, {}
    for q in order:
        level = trailing(q)
        source = gathered[q, level]
        for below in spans[q]:
            source = source + gathered[below, level]
        for below in spans[q]:
            source = source - dot3(sources[below], upper_block(below, level), True)
        sources[q] = source
        parts[q] = squared(source, upper_block(q, 0))
    solved = {}
    for q in reversed(order):
        solved[q] = parts[q]
        for up in range(q + 1, 8):
            if q in spans[up]:
                solved[q] = solved[q] - dot3(solved[up], upper_block(q, trailing(up)), False)
        xs[q] = solved[q]
    for level in range(4):
        q = (g // (1 << level)) * (1 << level) + (1 << level) - 1
        xpath[level] = xs[q] * exists(g, level).astype(f32)

    across = jnp.concatenate([xpath[0], xpath[1], xpath[2], xpath[3]], axis=1)
    x1 = ftop[1] - dot3(across, top_stack(1), False)
    x2 = ftop[2] - dot3(across, top_stack(2), False)
    x0 = ftop[0] - dot3(across, top_stack(0), False) - dot3(x1, top_block(0, 1), False)
    zown[0], zown[1], zown[6] = x0, x1, x2
    zown[2:6] = xpath[...]

    def share_z(i):
        to, device = mate(place, i)
        return remote(zown.at[pl.ds(0, 6)], zbuf.at[pl.ds(leaf, 6), my_cols], s_z.at[i], r_z.at[i], device)

    def z_from(i):
        view = zbuf.at[pl.ds(leaf, 6), at_cols(mate(place, i)[0])]
        return remote(zown.at[pl.ds(0, 6)], view, s_z.at[i], r_z.at[i], mate(place, i)[1])

    for i in range(1, 4):
        share_z(i).start()
    zbuf[pl.ds(leaf, 6), my_cols] = zown[0:6]

    def level_of(t):
        return sum(jnp.where((t + 1) % (1 << l) == 0, 1, 0) for l in range(1, 6))

    top_slots = (0, 1, 6, level_of(last))

    def share_top(m):
        return remote(zown.at[top_slots[m]], tout.at[my_cols], s_to.at[m], r_to.at[place], (4 * g + m, block))

    def top_from(k):
        return remote(zown.at[0], tout.at[at_cols(k)], s_to.at[0], r_to.at[k], worker(k))

    for m in range(4):

        @pl.when(not_own(m))
        def _(m=m):
            share_top(m).start()

    @pl.when(hub)
    def _():
        tout[my_cols] = zown[jnp.where(c == 2, 6, level_of(sn))]

    for i in range(1, 4):
        z_from(i).wait_recv()

    def back_piece(s):
        return remote(zbuf.at[s], o_leaf.at[s], s_back, r_back, (other, zo))

    def keep_piece(s):
        return pltpu.make_async_copy(zbuf.at[s], o_leaf.at[s], l_sem.at[0])

    def let_go(s):
        @pl.when(hub)
        def _():
            keep_piece(s).start()

        @pl.when(guest)
        def _():
            back_piece(s).start()

    def backward_step(s):
        b, d = leaf_block(s)
        z_at = jnp.concatenate([zbuf[s + 1], zbuf[slot_of(s, 1)], zbuf[slot_of(s, 2)]], axis=1)
        zbuf[s] = dot3(fwd[s] - dot3(z_at, b, False), d, False)

    backward_step(leaf - 1)

    def backward(j, carry):
        s = leaf - 2 - j
        backward_step(s)
        let_go(s + 1)
        return carry

    lax.fori_loop(0, leaf - 1, backward, 0)

    for k in range(4):

        @pl.when(not_me(k))
        def _(k=k):
            top_from(k).wait_recv()

    top_out = pltpu.make_async_copy(tout, o_top.at[0], l_sem.at[1])
    top_out.start()
    let_go(0)

    whole = pl.ds(0, leaf)

    def left(ssem, rows):
        b, d = blk.at[:, :, rows], dinv.at[:, rows]
        remote(b, b, ssem.at[0], r_in.at[0, 0, 0], (sn, zo)).wait_send()
        remote(d, d, ssem.at[1], r_in.at[0, 1, 0], (sn, zo)).wait_send()

    left(s_own.at[0], z)
    for i in range(3):
        if i < 2:
            top_z_all(i).wait_send()
        share_group(i).wait_send()
        share_part(i + 1).wait_send()
        share_z(i + 1).wait_send()
    for m in range(4):

        @pl.when(not_me(m))
        def _(m=m):
            share_rhs(m).wait_send()

        @pl.when(not_own(m))
        def _(m=m):
            share_top(m).wait_send()

    for i in range(1, 8):
        share_upper(i, 0).wait_send()
    for slot in range(1, 4):

        @pl.when(has_upper(g, slot))
        def _(slot=slot):
            for i in range(1, 8):
                share_upper(i, slot).wait_send()

    for level in range(4):

        @pl.when(exists(g, level))
        def _(level=level):
            for i in range(1, 8):
                share_contrib(i, level).wait_send()

    @pl.when(hub)
    def _():
        left(s_own.at[1], z)
        for to in range(4):
            left(s_fwd.at[to], z)
        to_guest.wait_send()
        pltpu.make_async_copy(zbuf.at[whole], o_leaf, l_sem.at[0]).wait()

    @pl.when(guest)
    def _():
        remote(rl, rin, s_rhs, r_rhs.at[0], (other, zo)).wait_send()
        everything = remote(zbuf.at[whole], o_leaf, s_back, r_back, (other, zo))
        everything.wait_send()
        everything.wait_recv()

    top_out.wait()


def local(rl, rt, lb, ld, st, tb, td):
    leaf, cols, w = rl.shape
    cc, quarter, chunks = cols // 4, w // 4, leaf // CHUNK
    any_spec = pl.BlockSpec(memory_space=pl.ANY)
    operands = [pltpu.with_memory_space_constraint(v, pltpu.HBM) for v in (st.T, rl, rt, lb, ld, tb, td)]
    dma = pltpu.SemaphoreType.DMA
    return pl.pallas_call(
        kernel,
        out_shape=(jax.ShapeDtypeStruct(rl.shape, f32), jax.ShapeDtypeStruct(rt.shape, f32)),
        in_specs=[any_spec] * 7,
        out_specs=(pl.BlockSpec(memory_space=pltpu.VMEM),) * 2,
        scratch_shapes=[
            pltpu.VMEM((leaf + 6, cols, w), f32),
            pltpu.VMEM((leaf, cols, w), f32),
            pltpu.VMEM((leaf, 3, 4, quarter, w), f32),
            pltpu.VMEM((leaf, 4, quarter, w), f32),
            pltpu.VMEM((leaf, cols, w), f32),
            pltpu.VMEM((leaf + 6, cols, w), f32),
            pltpu.VMEM((4, 6, 4, quarter, w), f32),
            pltpu.VMEM((4, cc, w), f32),
            pltpu.VMEM((4, 6, cc, w), f32),
            pltpu.VMEM((4, cc, w), f32),
            pltpu.VMEM((8, 4, cc, w), f32),
            pltpu.VMEM((8, 4, 4, quarter, w), f32),
            pltpu.VMEM((8, cc, w), f32),
            pltpu.VMEM((4, cc, w), f32),
            pltpu.VMEM((7, cc, w), f32),
            pltpu.VMEM((3, cc, w), f32),
            pltpu.VMEM((cols, w), f32),
            pltpu.VMEM(st.shape[::-1], jnp.int32),
            pltpu.SMEM(st.shape[::-1], jnp.int32),
            dma((2, 2)), dma((4, 2)), dma, dma, dma((4, 2, chunks)), dma((chunks,)), dma,
            dma((4,)), dma((4,)), dma((4,)), dma((4,)), dma((4,)), dma((4,)),
            dma((8, 4)), dma((8, 4)), dma((4,)), dma((4,)), dma((8, 4)), dma((8, 4)), dma((4,)), dma((4,)),
            dma((4,)), dma((4,)), dma, dma, dma((12,)),
        ],
        compiler_params=pltpu.CompilerParams(
            collective_id=0, has_side_effects=True, vmem_limit_bytes=24*1024*1024
        ),
        name="substitution",
    )(*operands)


def solution(mesh):
    return jax.shard_map(
        local,
        mesh=mesh,
        in_specs=(
            P("sn", "rhs", None),
            P("sn", "rhs", None),
            P("sn", None, "rhs", None),
            P("sn", "rhs", None),
            P("sn", None),
            P(None, "sn", "rhs", None),
            P("sn", "rhs", None),
        ),
        out_specs=(P("sn", "rhs", None), P("sn", "rhs", None)),
        check_vma=False,
    )
```
